128 devices in a mesh: ctx: 64 (over z, y, x_hi, core), chan: 2 (over x_lo).
Axes of the slice: x: 4 (x_hi: 2, x_lo: 2; x = x_hi * 2 + x_lo), y: 4, z: 4, core: 2. Of those that a mesh axis runs over, the one named last changes fastest.
Arguments:
- hidden: bfloat16 [16384, 2048], P('ctx'), may hold values from -6 to 6
- in_weight: bfloat16 [2048, 4096], P(None, 'chan'), may hold values from -0.125 to 0.125
- state_proj: bfloat16 [2, 16384, 128], P(None, 'ctx'), may hold values from -2.09375 to 2.09375
- log_decay: float32 [2, 16384, 64], P(None, 'ctx', 'chan'), may hold values from -1.6 to 0, as said below
- step_size: float32 [2, 16384, 64], P(None, 'ctx', 'chan'), may hold values from 0 to 1, as said below
- skip_gain: float32 [64], P('chan'), may hold values from 0.1 to 1.9
- cotangent: bfloat16 [16384, 4096], P('ctx', 'chan'), may hold values from -6 to 6
Outputs:
- layer_out: bfloat16 [16384, 4096], P('ctx', 'chan')
- input_grad: bfloat16 [16384, 2048], P('ctx', 'chan')
The draws below stay inside these ranges and needn't reach their ends.
Inputs may be any that keep to these rules, and one draw needn't show every extreme that they name: log_decay is never positive. step_size is positive.
All inputs are finite; a program needn't handle non-finite values.
Results may differ from the reference program's by a relative error of at most 0.014.
Values may be sent and summed in bfloat16 or wider, within the bound.
No kernel may reach another device: no remote copies, remote signals or barrier semaphores. Data moves between devices by JAX's collectives and lax.ppermute only.
A program may use at most 640 MiB of HBM per device.

```python
import math
import jax
import jax.numpy as jnp
from jax import lax

D = 2048
HEAD_TOTAL = 64
HEAD_DIM = 64
STATE = 64
GROUP = 128
TOK_DEV = 256
TOKEN_LENGTH = 16384
INNER = 4096


def selective_laws(key):
    random_keys = jax.random.split(jax.random.fold_in(key, 29), 8)
    fast_share = 0.3
    middle_top = 1.0 / 30.0
    choose = jax.random.uniform(random_keys[0], (2, HEAD_TOTAL))
    fast_base = jnp.exp(jax.random.uniform(random_keys[1], (2, HEAD_TOTAL), minval=math.log(1.0 / 50.0), maxval=math.log(1.0 / 30.0)))
    middle_base = jnp.exp(jax.random.uniform(random_keys[2], (2, HEAD_TOTAL), minval=math.log(0.01 / TOKEN_LENGTH), maxval=math.log(middle_top)))
    base_rate = jnp.where(choose < fast_share, fast_base, middle_base)
    block_count = TOKEN_LENGTH // TOK_DEV
    block_factor = jnp.exp(jax.random.uniform(random_keys[3], (2, block_count, 1, HEAD_TOTAL), minval=math.log(0.5), maxval=math.log(2.0)))
    block_factor = jnp.broadcast_to(block_factor, (2, block_count, TOK_DEV, HEAD_TOTAL)).reshape(2, TOKEN_LENGTH, HEAD_TOTAL)
    roughness = jnp.exp(jax.random.uniform(random_keys[4], (2, TOKEN_LENGTH, HEAD_TOTAL), minval=math.log(0.5), maxval=math.log(2.0)))
    decay_speed = base_rate[:, None, :] * block_factor * roughness
    spike_position = jax.random.randint(random_keys[5], (2, 2), 0, TOKEN_LENGTH)
    token_positions = jnp.arange(TOKEN_LENGTH)
    spike_events = jnp.sum((token_positions[None, None, :] == spike_position[:, :, None]).astype(jnp.float32), axis=1)
    spike_loss = jax.random.uniform(random_keys[6], (2, HEAD_TOTAL), minval=0.22, maxval=0.69)
    decay_values = -decay_speed - spike_events[:, :, None] * spike_loss[:, None, :]
    step_rough = jnp.exp(jax.random.uniform(random_keys[7], (2, TOKEN_LENGTH, HEAD_TOTAL), minval=math.log(0.7), maxval=math.log(1.4)))
    step_sizes = jnp.sqrt(2.0 * decay_speed + 4.0 / TOKEN_LENGTH) * step_rough
    return (decay_values.astype(jnp.float32), step_sizes.astype(jnp.float32))


def draw_log_decay(key, part):
    return selective_laws(key)[0]


def draw_step_size(key, part):
    return selective_laws(key)[1]


def steps_of(stream_key, extent, shards, least, high):
    gain, own = 1.0, jax.random.fold_in(stream_key, 6)
    for position, blocks in shards:
        steps = jnp.exp(jax.random.uniform(jax.random.fold_in(own, position), (blocks,), jnp.float32, least / len(shards), high / len(shards)))
        gain = gain * jnp.repeat(steps, extent[position] // blocks).reshape([-1 if axis == position else 1 for axis in range(len(extent))])
    return gain


def scatter_about(key, extent, deviation, reach, shards=(), held_as=jnp.bfloat16):
    level = steps_of(key, extent, shards, -0.22, 0.18) if shards else 1.0
    entries = jax.random.normal(key, extent, jnp.float32) * deviation * level
    return jnp.minimum(jnp.maximum(entries, -reach), reach).astype(held_as)


def setup_inputs(seed: int = 0) -> dict:
    arg_keys = jax.random.split(jax.random.key(seed), 8)
    hidden = scatter_about(arg_keys[0], (TOKEN_LENGTH, D), 1.0, 6.0, ((0, 64),))
    in_weight = scatter_about(arg_keys[1], (D, INNER), D ** -0.5, 0.125, ((1, 2),))
    state_proj = scatter_about(arg_keys[2], (2, TOKEN_LENGTH, 2 * STATE), 0.35, 2.09375, ((1, 64),))
    log_decay = draw_log_decay(jax.random.fold_in(arg_keys[7], 71), 0)
    step_size = draw_step_size(jax.random.fold_in(arg_keys[7], 71), 0)
    skip_gain = jnp.clip(1.0 + 0.18 * jax.random.normal(arg_keys[5], (HEAD_TOTAL,), jnp.float32), 0.1, 1.9)
    cotangent = scatter_about(arg_keys[6], (TOKEN_LENGTH, INNER), 1.0, 6.0, ((0, 64), (1, 2)))
    return {"hidden": hidden, "in_weight": in_weight, "state_proj": state_proj, "log_decay": log_decay, "step_size": step_size, "skip_gain": skip_gain, "cotangent": cotangent}


def block_scan(query_rows, key_rows, value_rows, weights, decay_values, exclusive):
    length = query_rows.shape[0]
    blocks = length // GROUP
    head_count = value_rows.shape[1]
    head_width = value_rows.shape[2]
    state_width = query_rows.shape[1]

    def advance(states, members):
        query_blk, key_blk, value_blk, weight_blk, decay_blk = members
        cumul = jnp.cumsum(decay_blk, axis=0)
        if exclusive:
            level = cumul - decay_blk
        else:
            level = cumul
        affinity = jnp.dot(query_blk, key_blk.T, preferred_element_type=jnp.float32)
        differ = level.T[:, :, None] - level.T[:, None, :]
        row_index = lax.broadcasted_iota(jnp.int32, (GROUP, GROUP), 0)
        col_index = lax.broadcasted_iota(jnp.int32, (GROUP, GROUP), 1)
        kernel = jnp.exp(jnp.where((row_index >= col_index)[None], differ, -jnp.inf))
        mixing = (affinity[None] * kernel * weight_blk.T[:, None, :]).astype(jnp.bfloat16)
        within = jnp.einsum("hts,shp->thp", mixing.astype(jnp.float32), value_blk.astype(jnp.float32), precision=lax.Precision.HIGHEST)
        rounded = states.astype(jnp.bfloat16).astype(jnp.float32)
        carried = jnp.exp(level)[:, :, None] * jnp.einsum("tn,hpn->thp", query_blk.astype(jnp.float32), rounded, precision=lax.Precision.HIGHEST)
        closing = cumul[-1]
        fading = jnp.exp(closing[None, :] - level) * weight_blk
        weighted = (fading[:, :, None] * key_blk.astype(jnp.float32)[:, None, :]).astype(jnp.bfloat16).astype(jnp.float32)
        states = jnp.exp(closing)[:, None, None] * states + jnp.einsum("shn,shp->hpn", weighted, value_blk.astype(jnp.float32), precision=lax.Precision.HIGHEST)
        return states, within + carried

    members = tuple(member.reshape((blocks, GROUP) + member.shape[1:]) for member in (query_rows, key_rows, value_rows, weights, decay_values))
    initial = jnp.zeros((head_count, head_width, state_width), jnp.float32)
    _, results = lax.scan(advance, initial, members)
    return results.reshape(length, head_count, head_width)


def reverse_rows(array):
    return jnp.flip(array, 0)


def reference(hidden, in_weight, state_proj, log_decay, step_size, skip_gain, cotangent):
    length = hidden.shape[0]
    u_fwd = jnp.dot(hidden, in_weight, preferred_element_type=jnp.float32).astype(jnp.bfloat16)
    u_rev = jnp.dot(hidden[:, ::-1], in_weight, preferred_element_type=jnp.float32).astype(jnp.bfloat16)
    keys_f = state_proj[0, :, :STATE]
    query_f = state_proj[0, :, STATE:]
    keys_r = state_proj[1, :, :STATE]
    query_r = state_proj[1, :, STATE:]
    gains = skip_gain[None, :, None]
    fwd_values = u_fwd.reshape(length, HEAD_TOTAL, HEAD_DIM)
    rev_values = u_rev.reshape(length, HEAD_TOTAL, HEAD_DIM)
    scan_ff = block_scan(query_f, keys_f, fwd_values, step_size[0], log_decay[0], False)
    y_fwd = scan_ff + gains * fwd_values.astype(jnp.float32)
    scan_rf = reverse_rows(block_scan(reverse_rows(query_r), reverse_rows(keys_r), reverse_rows(rev_values), reverse_rows(step_size[1]), reverse_rows(log_decay[1]), False))
    y_rev = (scan_rf + gains * rev_values.astype(jnp.float32)).astype(jnp.bfloat16)
    layer_out = (y_fwd.reshape(length, INNER) + y_rev.reshape(length, INNER)[:, ::-1].astype(jnp.float32)).astype(jnp.bfloat16)
    cot_values = cotangent.reshape(length, HEAD_TOTAL, HEAD_DIM)
    rc_cotangent = cotangent[:, ::-1].reshape(length, HEAD_TOTAL, HEAD_DIM)
    unit = jnp.ones_like(step_size[0])
    scan_fb = reverse_rows(block_scan(reverse_rows(keys_f), reverse_rows(query_f), reverse_rows(cot_values), unit, reverse_rows(log_decay[0]), True))
    grad_f = (step_size[0][:, :, None] * scan_fb + gains * cot_values.astype(jnp.float32)).astype(jnp.bfloat16)
    scan_rb = block_scan(keys_r, query_r, rc_cotangent, unit, log_decay[1], True)
    grad_r = (step_size[1][:, :, None] * scan_rb + gains * rc_cotangent.astype(jnp.float32)).astype(jnp.bfloat16)
    direct = jnp.dot(grad_f.reshape(length, INNER), in_weight.T, preferred_element_type=jnp.float32)
    mirrored = jnp.dot(grad_r.reshape(length, INNER), in_weight.T, preferred_element_type=jnp.float32)
    input_grad = (direct + mirrored[:, ::-1]).astype(jnp.bfloat16)
    return layer_out, input_grad
```

```python
import jax
import jax.numpy as jnp
from jax import lax
from jax.experimental import pallas as pl
from jax.experimental.pallas import tpu as pltpu
from jax.sharding import PartitionSpec as P

F32 = jnp.float32
BF16 = jnp.bfloat16
ROWS = 256
WIDTH = 2048
LANES = 256
STEPS = WIDTH // LANES
HEAD = 64
STATE = 64
SUB = 64
TILE = 128
SLICES = WIDTH // TILE
BODY = 4 * STATE
FULL = BODY + 16
FF, RF, FB, RB = 0, 1, 2, 3
FORWARD = (True, False, False, True)
NT = (((1,), (1,)), ((), ()))


def mm(a, b):
    return jnp.dot(a, b, preferred_element_type=F32)


def mm_nt(a, b):
    return lax.dot_general(a, b, NT, preferred_element_type=F32)


def iota(shape, dim):
    return lax.broadcasted_iota(jnp.int32, shape, dim)


def split3(x):
    high = x.astype(BF16)
    rest = x - high.astype(F32)
    middle = rest.astype(BF16)
    low = (rest - middle.astype(F32)).astype(BF16)
    return high, middle, low


def exact_mm(ones, x):
    high, middle, low = split3(x)
    return mm(ones, high) + mm(ones, middle) + mm(ones, low)


def pair(x):
    high = x.astype(BF16)
    low = (x - high.astype(F32)).astype(BF16)
    return jnp.concatenate([high, low], axis=1)


def exchange_matrix(n):
    return (iota((n, n), 0) + iota((n, n), 1) == n - 1).astype(BF16)


def spread(rows, base, block, mirrored):
    row = iota((rows, LANES), 0) & 127
    head = block * (LANES // HEAD) + iota((rows, LANES), 1) // HEAD
    if mirrored:
        head = WIDTH // HEAD - 1 - head
    return (row == base + head).astype(BF16)


def picks(n, offset):
    row = iota((n, TILE), 0) & (STATE - 1)
    return (iota((n, TILE), 1) == offset + row).astype(BF16)


def place():
    index = lax.axis_index("ctx")
    return index & 1, (index >> 1) & 1, (index >> 2) & 3, index >> 4


def project_kernel(hidden, weight, proj, pack, cot, u_f, u_r, states, both, scale, keys):
    step = pl.program_id(0)

    @pl.when(step == 0)
    def _():
        flip = exchange_matrix(LANES)
        for b in range(STEPS):
            block = hidden[:, b * LANES : (b + 1) * LANES]
            back = STEPS - 1 - b
            both[0:ROWS, b * LANES : (b + 1) * LANES] = block
            both[ROWS : 2 * ROWS, back * LANES : (back + 1) * LANES] = mm(block, flip).astype(BF16)
        table = pack[0:ROWS, :]
        lane = iota((ROWS, TILE), 1)
        decay = jnp.where(lane < 64, table, 0.0)
        lower = (iota((ROWS, ROWS), 0) >= iota((ROWS, ROWS), 1)).astype(BF16)
        total = exact_mm(lower, decay)
        last = total[ROWS - 1 : ROWS, :]
        weight_of = pltpu.roll(table, 64, 1)
        values = jnp.where(
            lane < 32,
            jnp.exp(last - total) * weight_of,
            jnp.where(
                lane < 64, jnp.exp(total - decay) * weight_of, pltpu.roll(jnp.exp(total), 64, 1)
            ),
        )
        scale[...] = pair(values)
        keys[0] = mm_nt(picks(STATE, 0), proj[0]).astype(BF16)
        keys[1] = mm_nt(picks(STATE, 0), proj[1]).astype(BF16)
        keys[2] = mm_nt(picks(STATE, STATE), proj[0]).astype(BF16)

    u = mm(both[...], weight[...]).astype(BF16)
    u_f[...] = u[0:ROWS]
    u_r[...] = u[ROWS : 2 * ROWS]
    values = (u[0:ROWS].astype(F32), u[ROWS : 2 * ROWS].astype(F32), cot[...].astype(F32))
    for scan in range(3):
        wide = mm(scale[...], spread(2 * TILE, 32 * scan, step, False))
        state = mm(keys[scan], (values[scan] * wide).astype(BF16)).astype(BF16)
        for j in range(LANES // TILE):
            states[j, scan * STATE : (scan + 1) * STATE, :] = state[:, j * TILE : (j + 1) * TILE]


def project(hidden, weight, proj, pack, cot):
    columns = pl.BlockSpec((ROWS, LANES), lambda i: (0, i))
    return pl.pallas_call(
        project_kernel,
        grid=(STEPS,),
        in_specs=[
            pl.BlockSpec((ROWS, WIDTH), lambda i: (0, 0)),
            pl.BlockSpec((WIDTH, LANES), lambda i: (0, i)),
            pl.BlockSpec((2, ROWS, TILE), lambda i: (0, 0, 0)),
            pl.BlockSpec((ROWS + 8, TILE), lambda i: (0, 0)),
            columns,
        ],
        out_specs=[
            columns,
            columns,
            pl.BlockSpec((LANES // TILE, 3 * STATE, TILE), lambda i: (i, 0, 0)),
        ],
        out_shape=[
            jax.ShapeDtypeStruct((ROWS, WIDTH), BF16),
            jax.ShapeDtypeStruct((ROWS, WIDTH), BF16),
            jax.ShapeDtypeStruct((SLICES, 3 * STATE, TILE), BF16),
        ],
        scratch_shapes=[
            pltpu.VMEM((2 * ROWS, WIDTH), BF16),
            pltpu.VMEM((ROWS, 2 * TILE), BF16),
            pltpu.VMEM((3, STATE, ROWS), BF16),
        ],
        cost_estimate=pl.CostEstimate(
            flops=4 * ROWS * WIDTH * WIDTH, bytes_accessed=14 << 20, transcendentals=0
        ),
        name="project",
    )(hidden, weight, proj, pack, cot)


def mirror_kernel(cot, proj, pack, other_pack, states, keep, send):
    core, _, _, _ = place()
    decay = jnp.where(iota((ROWS, TILE), 1) < 64, other_pack[0:ROWS, :], 0.0)
    own = jnp.where(iota((ROWS, TILE), 1) < 64, pack[0:ROWS, :], 0.0)
    lower = (iota((ROWS, ROWS), 0) >= iota((ROWS, ROWS), 1)).astype(BF16)
    total = exact_mm(lower, decay)
    last = total[ROWS - 1 : ROWS, :]
    scale = pair(jnp.exp(last - total + decay))
    keys = mm_nt(picks(STATE, STATE), proj[1]).astype(BF16)
    own_last = exact_mm(jnp.ones((16, ROWS), BF16), own)
    other_last = jnp.broadcast_to(last, (16, TILE))
    row, lane = iota((16, TILE), 0), iota((16, TILE), 1)
    scan, part = row // 3, row % 3

    def parts(x, wanted):
        high, middle, low = split3(jnp.exp(x))
        chosen = jnp.where(
            part == 0, high.astype(F32), jnp.where(part == 1, middle.astype(F32), low.astype(F32))
        )
        return jnp.where(wanted, chosen, 0.0).astype(BF16)

    direction = lane // 32
    own_rows = parts(own_last, (scan < 3) & (direction == (scan == RF).astype(jnp.int32)))
    other_rows = parts(other_last, (scan == RB) & (direction == 1))
    head_row = iota((TILE, LANES), 0) & 31
    for b in range(STEPS):
        head = b * (LANES // HEAD) + iota((TILE, LANES), 1) // HEAD
        straight = (head_row == head).astype(BF16)
        turned = (head_row == WIDTH // HEAD - 1 - head).astype(BF16)
        decays = (mm(own_rows, straight) + mm(other_rows, turned)).astype(BF16)
        wide = mm(scale, spread(2 * TILE, 32, b, True))
        block = cot[:, b * LANES : (b + 1) * LANES].astype(F32)
        state = mm(keys, (block * wide).astype(BF16)).astype(BF16)
        for j in range(LANES // TILE):
            s = b * (LANES // TILE) + j
            half, at = s // (SLICES // 2), s % (SLICES // 2)
            columns = slice(j * TILE, (j + 1) * TILE)

            def write(out):
                out[at, 0 : 3 * STATE, :] = states[s]
                out[at, 3 * STATE : BODY, :] = state[:, columns]
                out[at, BODY:FULL, :] = decays[:, columns]

            @pl.when(core == half)
            def _():
                write(keep)

            @pl.when(core != half)
            def _():
                write(send)


def whole(kernel, outs, args, scratch=(), name=None, flops=0):
    bytes_accessed = sum(a.size * a.dtype.itemsize for a in args)
    bytes_accessed += sum(2 * o.size for o in outs)
    return pl.pallas_call(
        kernel,
        out_shape=outs,
        in_specs=[pl.BlockSpec(memory_space=pltpu.VMEM)] * len(args),
        out_specs=[pl.BlockSpec(memory_space=pltpu.VMEM)] * len(outs),
        scratch_shapes=list(scratch),
        cost_estimate=pl.CostEstimate(
            flops=flops, bytes_accessed=bytes_accessed, transcendentals=0
        ),
        name=name,
    )(*args)


def shape(*dims):
    return jax.ShapeDtypeStruct(dims, BF16)


def read_decays(tile):
    tile = tile.astype(F32)
    return [
        tile[3 * i : 3 * i + 1] + tile[3 * i + 1 : 3 * i + 2] + tile[3 * i + 2 : 3 * i + 3]
        for i in range(tile.shape[0] // 4)
    ]


def decay_rows(decays):
    row = iota((16, TILE), 0)
    out = jnp.zeros((16, TILE), F32)
    for i, d in enumerate(decays):
        for j, p in enumerate(split3(d)):
            out = jnp.where(row == 3 * i + j, p.astype(F32), out)
    return out.astype(BF16)


def rows_of(scan):
    return slice(scan * STATE, (scan + 1) * STATE)


def pair_total(own, got, at, first, out, to):
    mine, theirs = read_decays(own[at, BODY:FULL, :]), read_decays(got[at, BODY:FULL, :])
    for scan in range(4):
        early = first if FORWARD[scan] else 1.0 - first
        alpha = early * theirs[scan] + (1.0 - early)
        beta = early + (1.0 - early) * mine[scan]
        out[to, rows_of(scan), :] = (
            alpha * own[at, rows_of(scan), :].astype(F32)
            + beta * got[at, rows_of(scan), :].astype(F32)
        ).astype(BF16)
    out[to, BODY:FULL, :] = decay_rows([a * b for a, b in zip(mine, theirs)])


def pair_carry(own, got, at, first, carry, mine, theirs, scan):
    early = first if FORWARD[scan] else 1.0 - first
    here = (1.0 - early) * (theirs[scan] * carry + got[at, rows_of(scan), :].astype(F32))
    here = here + early * carry
    there = early * (mine[scan] * carry + own[at, rows_of(scan), :].astype(F32))
    there = there + (1.0 - early) * carry
    return here.astype(BF16), there.astype(BF16)


def core_up_kernel(own, got, keep, send):
    core, x, _, _ = place()
    first = 1.0 - core.astype(F32)

    @pl.loop(0, 4)
    def _(j):
        pair_total(own, got, x * 4 + j, first, keep, j)
        pair_total(own, got, (1 - x) * 4 + j, first, send, j)


def x_up_kernel(own, got, *outs):
    _, x, y, _ = place()
    first = 1.0 - x.astype(F32)
    for k in range(4):
        pair_total(own, got, (y + k) & 3, first, outs[k], 0)


def y_total_kernel(a0, a1, a2, a3, z1, z2, z3, stack, total):
    _, _, y, z = place()
    for k, a in enumerate((a0, a1, a2, a3)):
        stack[(y - k) & 3] = a[0]
    decays = [read_decays(stack[p, BODY:FULL, :]) for p in range(4)]
    for scan in range(4):
        order = (0, 1, 2, 3) if FORWARD[scan] else (3, 2, 1, 0)
        t = stack[order[0], rows_of(scan), :].astype(F32)
        for p in order[1:]:
            t = decays[p][scan] * t + stack[p, rows_of(scan), :].astype(F32)
        total[rows_of(scan), :] = t.astype(BF16)
    product = [decays[0][s] * decays[1][s] * decays[2][s] * decays[3][s] for s in range(4)]
    later = decay_rows([product[FF], product[RB]])
    earlier = decay_rows([product[RF], product[FB]])
    for k, out in enumerate((z1, z2, z3)):

        @pl.when(z + k + 1 < 4)
        def _():
            out[0:STATE, :] = total[rows_of(FF), :]
            out[STATE : 2 * STATE, :] = total[rows_of(RB), :]
            out[2 * STATE :, :] = later

        @pl.when(z + k + 1 >= 4)
        def _():
            out[0:STATE, :] = total[rows_of(RF), :]
            out[STATE : 2 * STATE, :] = total[rows_of(FB), :]
            out[2 * STATE :, :] = earlier


def z_carry_kernel(a0, a1, a2, a3, q1, q2, q3, d0, d1, d2, d3, stack, out):
    _, _, y, z = place()
    for k, a in enumerate((a0, a1, a2, a3)):
        stack[(y - k) & 3] = a[0]
    decays = [read_decays(stack[p, BODY:FULL, :]) for p in range(4)]
    got = (q1, q2, q3)
    plane = [read_decays(q[2 * STATE :, :]) for q in got]
    before = [(z >= k).astype(F32) for k in (1, 2, 3)]
    for scan in range(4):
        half = 0 if scan in (FF, RF) else 1
        part = [q[half * STATE : (half + 1) * STATE, :].astype(F32) for q in got]
        d = [p[half] for p in plane]
        if FORWARD[scan]:
            m = before
            order, positions = (0, 1, 2), (0, 1, 2, 3)
        else:
            m = [1.0 - b for b in before]
            order, positions = (2, 1, 0), (3, 2, 1, 0)
        i, j, k = order
        c = m[i] * (part[i] + d[i] * (m[j] * (part[j] + d[j] * (m[k] * part[k]))))
        for p in positions:
            out[p, rows_of(scan), :] = c.astype(BF16)
            if p != positions[-1]:
                c = decays[p][scan] * c + stack[p, rows_of(scan), :].astype(F32)
    for k, d in enumerate((d0, d1, d2, d3)):
        d[...] = out[(y - k) & 3]


def x_down_kernel(c0, c1, c2, c3, own, got, keep, send):
    _, x, y, _ = place()
    first = 1.0 - x.astype(F32)
    for k, c in enumerate((c0, c1, c2, c3)):
        at = (y + k) & 3
        mine, theirs = read_decays(own[at, BODY:FULL, :]), read_decays(got[at, BODY:FULL, :])
        for scan in range(4):
            here, there = pair_carry(
                own, got, at, first, c[rows_of(scan), :].astype(F32), mine, theirs, scan
            )
            keep[at, rows_of(scan), :] = here
            send[at, rows_of(scan), :] = there


def core_down_kernel(c_own, c_got, own, got, f_keep, f_send, b_same, b_cross, r_same, r_cross):
    core, x, _, _ = place()
    first = 1.0 - core.astype(F32)

    @pl.loop(0, 4)
    def _(j):
        for carry, side in ((c_own, x), (c_got, 1 - x)):
            at = side * 4 + j
            mine, theirs = read_decays(own[at, BODY:FULL, :]), read_decays(got[at, BODY:FULL, :])
            for scan, here_out, there_out, row in (
                (FF, f_keep, f_send, 0),
                (FB, f_keep, f_send, STATE),
                (RB, b_same, b_cross, 0),
                (RF, r_same, r_cross, 0),
            ):
                here, there = pair_carry(
                    own,
                    got,
                    at,
                    first,
                    carry[j, rows_of(scan), :].astype(F32),
                    mine,
                    theirs,
                    scan,
                )
                here_out[at, row : row + STATE, :] = here
                there_out[at, row : row + STATE, :] = there


def ctx_permute(x, target):
    return lax.ppermute(x, "ctx", [(i, target(i)) for i in range(64)])


def core_swap(x):
    return ctx_permute(x, lambda i: i ^ 1)


def x_swap(x):
    return ctx_permute(x, lambda i: i ^ 2)


def y_shift(x, k):
    return ctx_permute(x, lambda i: (i & ~12) | ((i + 4 * k) & 12))


def z_shift(x, k):
    return ctx_permute(x, lambda i: (i + 16 * k) & 63)


def chan_swap(x):
    return lax.ppermute(x, "chan", [(0, 1), (1, 0)])


def cross_swap(x):
    return lax.ppermute(x, ("ctx", "chan"), [(i, i ^ 3) for i in range(128)])


def carries(keep1, send1):
    slices = SLICES // 2
    got1 = core_swap(send1)
    keep2, send2 = whole(
        core_up_kernel, [shape(4, FULL, TILE)] * 2, (keep1, got1), name="core_up"
    )
    got2 = x_swap(send2)
    tops = whole(x_up_kernel, [shape(1, FULL, TILE)] * 4, (keep2, got2), name="x_up")
    row = [tops[0]] + [y_shift(tops[k], k) for k in (1, 2, 3)]
    stack = pltpu.VMEM((4, FULL, TILE), BF16)
    planes = whole(
        y_total_kernel,
        [shape(2 * STATE + 16, TILE)] * 3,
        row,
        [stack, pltpu.VMEM((BODY, TILE), BF16)],
        name="y_total",
    )
    other = [z_shift(planes[k - 1], k) for k in (1, 2, 3)]
    down = whole(
        z_carry_kernel,
        [shape(BODY, TILE)] * 4,
        row + other,
        [stack, pltpu.VMEM((4, BODY, TILE), BF16)],
        name="z_carry",
    )
    down = [down[0]] + [y_shift(down[k], -k) for k in (1, 2, 3)]
    keep3, send3 = whole(
        x_down_kernel, [shape(4, BODY, TILE)] * 2, [*down, keep2, got2], name="x_down"
    )
    got3 = x_swap(send3)
    f_keep, f_send, b_same, b_cross, r_same, r_cross = whole(
        core_down_kernel,
        [shape(slices, 2 * STATE, TILE)] * 2 + [shape(slices, STATE, TILE)] * 4,
        (keep3, got3, keep1, got1),
        name="core_down",
    )
    return (
        (f_keep, core_swap(f_send)),
        (chan_swap(b_same), cross_swap(b_cross)),
        (chan_swap(r_same), cross_swap(r_cross)),
    )


def prepare(tables, proj_of, forward, exclusive, with_weight, in_scale, out_scale, rows_scale):
    lane = iota((ROWS, TILE), 1)
    first, second = tables
    table = jnp.where(lane & 32 == 0, first[0:ROWS, :], second[0:ROWS, :])
    decay = jnp.where(lane < 64, table, 0.0)
    weight = pltpu.roll(table, 64, 1)
    row, column = iota((ROWS, ROWS), 0), iota((ROWS, ROWS), 1)
    same = row // SUB == column // SUB
    total = exact_mm((same & (row >= column)).astype(BF16), decay)
    full = exact_mm(same.astype(BF16), decay)

    def level(i):
        c = total if forward[i] else full - total + decay
        return c - decay if exclusive[i] else c

    rise = jnp.where(lane < 32, level(0), level(1)) - 0.5 * full
    in_scale[...] = pair(jnp.exp(-rise) * weight if with_weight else jnp.exp(-rise))
    out_scale[...] = pair(jnp.exp(rise) if with_weight else jnp.exp(rise) * weight)
    small = iota((16, TILE), 0)
    tail = jnp.where(
        iota((8, TILE), 1) & 32 == 0, first[ROWS : ROWS + 8, :], second[ROWS : ROWS + 8, :]
    )
    half = jnp.exp(0.5 * full)
    values = jnp.broadcast_to(tail[0:1], (16, TILE))
    for b in range(ROWS // SUB):
        values = jnp.where(small == b, half[b * SUB : b * SUB + 1], values)
    rows_scale[...] = pair(values)


def prepare_matrices(proj, query_at, forward, inside, query, keys):
    key_at = STATE - query_at
    row, column = iota((ROWS, ROWS), 0), iota((ROWS, ROWS), 1)
    same = row // SUB == column // SUB
    order = (row >= column) if forward else (row <= column)
    tiled_query = mm_nt(proj, picks(ROWS, query_at))
    tiled_keys = mm_nt(picks(ROWS, key_at), proj)
    q = jnp.where(iota((ROWS, TILE), 1) // STATE == query_at // STATE, proj.astype(F32), 0.0)
    swapped = pltpu.roll(proj.astype(F32), STATE, 1).astype(BF16)
    affinity = mm_nt(q.astype(BF16), swapped)
    inside[...] = jnp.where(same & order, affinity, 0.0).astype(BF16)
    query[...] = jnp.where(same, tiled_query, 0.0).astype(BF16)
    keys[...] = jnp.where(same, tiled_keys, 0.0).astype(BF16)


def scan_block(values, carry, forward, lanes, in_scale, out_scale, rows_scale, mats):
    inside, query, keys = mats
    wide = mm(in_scale[...], lanes)
    small = mm(rows_scale[...], lanes)
    out = mm(out_scale[...], lanes)
    scaled = (values * wide).astype(BF16)
    fresh = mm(keys[...], scaled)
    blocks = ROWS // SUB
    entering = [None] * blocks
    state = carry
    for b in range(blocks) if forward else range(blocks - 1, -1, -1):
        half = small[b : b + 1]
        met = half * state
        entering[b] = met.astype(BF16)
        state = half * (met + fresh[b * SUB : (b + 1) * SUB])
    scan = mm(inside[...], scaled) + mm(query[...], jnp.concatenate(entering, axis=0))
    return scan * out + small[8:9] * values


def carry_block(keep, got, core, block, row):
    mine = (core == block // (STEPS // 2)).astype(F32)
    parts = [
        mine * keep[j, row : row + STATE, :].astype(F32)
        + (1.0 - mine) * got[j, row : row + STATE, :].astype(F32)
        for j in range(LANES // TILE)
    ]
    return jnp.concatenate(parts, axis=1)


def grads_kernel(
    cot, other_cot, proj, pack, f_keep, f_got, b_keep, b_got, du_f, du_r, *scratch
):
    step = pl.program_id(0)
    core, _, _, _ = place()
    in_scale, out_scale, rows_scale = scratch[0:3]
    straight, turned = scratch[3:6], scratch[6:9]

    @pl.when(step == 0)
    def _():
        tables = (pack, pack)
        prepare(
            tables, proj, (False, True), (True, True), False, in_scale, out_scale, rows_scale
        )
        prepare_matrices(proj[0], 0, False, *straight)
        prepare_matrices(proj[1], 0, True, *turned)

    back = STEPS - 1 - step
    du_f[...] = scan_block(
        cot[...].astype(F32),
        carry_block(f_keep, f_got, core, step, STATE),
        False,
        spread(2 * TILE, 0, step, False),
        in_scale,
        out_scale,
        rows_scale,
        straight,
    ).astype(BF16)
    mirrored = scan_block(
        other_cot[...].astype(F32),
        carry_block(b_keep, b_got, core, back, 0),
        True,
        spread(2 * TILE, 32, back, True),
        in_scale,
        out_scale,
        rows_scale,
        turned,
    ).astype(BF16)
    du_r[...] = mm(mirrored, exchange_matrix(LANES)).astype(BF16)


def layer_kernel(
    u_f, other_u, proj, pack, other_pack, f_keep, f_got, r_keep, r_got, out, *scratch
):
    step = pl.program_id(0)
    core, _, _, _ = place()
    in_scale, out_scale, rows_scale = scratch[0:3]
    straight, turned = scratch[3:6], scratch[6:9]

    @pl.when(step == 0)
    def _():
        tables = (pack, other_pack)
        prepare(
            tables, proj, (True, False), (False, False), True, in_scale, out_scale, rows_scale
        )
        prepare_matrices(proj[0], STATE, True, *straight)
        prepare_matrices(proj[1], STATE, False, *turned)

    back = STEPS - 1 - step
    y_f = scan_block(
        u_f[...].astype(F32),
        carry_block(f_keep, f_got, core, step, 0),
        True,
        spread(2 * TILE, 0, step, False),
        in_scale,
        out_scale,
        rows_scale,
        straight,
    )
    y_r = scan_block(
        other_u[...].astype(F32),
        carry_block(r_keep, r_got, core, back, 0),
        False,
        spread(2 * TILE, 32, back, False),
        in_scale,
        out_scale,
        rows_scale,
        turned,
    ).astype(BF16)
    out[...] = (y_f + mm(y_r, exchange_matrix(LANES))).astype(BF16)


def scan_scratch():
    square = pltpu.VMEM((ROWS, ROWS), BF16)
    wide = pltpu.VMEM((ROWS, 2 * TILE), BF16)
    return [wide, wide, pltpu.VMEM((16, 2 * TILE), BF16)] + [square] * 6


def carry_specs(rows, mirrored):
    half = STEPS // 2
    if mirrored:
        return [pl.BlockSpec((LANES // TILE, rows, TILE), lambda i: ((STEPS - 1 - i) % half, 0, 0))] * 2
    return [pl.BlockSpec((LANES // TILE, rows, TILE), lambda i: (i % half, 0, 0))] * 2


COLUMNS = pl.BlockSpec((ROWS, LANES), lambda i: (0, i))
MIRRORED = pl.BlockSpec((ROWS, LANES), lambda i: (0, STEPS - 1 - i))
PROJ = pl.BlockSpec((2, ROWS, TILE), lambda i: (0, 0, 0))
PACK = pl.BlockSpec((ROWS + 8, TILE), lambda i: (0, 0))
SCAN_COST = pl.CostEstimate(flops=10 << 30, bytes_accessed=6 << 20, transcendentals=0)


def grads(cot, other_cot, proj, pack, f_carry, b_carry):
    return pl.pallas_call(
        grads_kernel,
        grid=(STEPS,),
        in_specs=[COLUMNS, MIRRORED, PROJ, PACK]
        + carry_specs(2 * STATE, False)
        + carry_specs(STATE, True),
        out_specs=[COLUMNS, COLUMNS],
        out_shape=[shape(ROWS, WIDTH), shape(ROWS, WIDTH)],
        scratch_shapes=scan_scratch(),
        cost_estimate=SCAN_COST,
        name="grads",
    )(cot, other_cot, proj, pack, *f_carry, *b_carry)


def layer(u_f, other_u, proj, pack, other_pack, f_carry, r_carry):
    return pl.pallas_call(
        layer_kernel,
        grid=(STEPS,),
        in_specs=[COLUMNS, MIRRORED, PROJ, PACK, PACK]
        + carry_specs(2 * STATE, False)
        + carry_specs(STATE, True),
        out_specs=COLUMNS,
        out_shape=shape(ROWS, WIDTH),
        scratch_shapes=scan_scratch(),
        cost_estimate=SCAN_COST,
        name="layer",
    )(u_f, other_u, proj, pack, other_pack, *f_carry, *r_carry)


def back_kernel(half, du_f, du_r, direct, mirrored, *rest):
    total = mm_nt(du_f[...], direct[...])
    turn = mm_nt(du_r[...], mirrored[...])
    high = turn.astype(BF16)
    low = (turn - high.astype(F32)).astype(BF16)
    flip = exchange_matrix(LANES)
    total = total + mm(high, flip) + mm(low, flip)
    if len(rest) == 2:
        total = total + rest[0][...].astype(F32)
    rest[-1][...] = total.astype(rest[-1].dtype)


def back(half, du_f, du_r, weight, dtype):
    steps = STEPS // 2
    spec = pltpu.PrefetchScalarGridSpec(
        num_scalar_prefetch=1,
        grid=(steps,),
        in_specs=[
            pl.BlockSpec((ROWS, WIDTH), lambda i, h: (0, 0)),
            pl.BlockSpec((ROWS, WIDTH), lambda i, h: (0, 0)),
            pl.BlockSpec((LANES, WIDTH), lambda i, h: (h[0] * steps + i, 0)),
            pl.BlockSpec((LANES, WIDTH), lambda i, h: (STEPS - 1 - h[0] * steps - i, 0)),
        ],
        out_specs=pl.BlockSpec((ROWS, LANES), lambda i, h: (0, i)),
    )
    return pl.pallas_call(
        back_kernel,
        grid_spec=spec,
        out_shape=jax.ShapeDtypeStruct((ROWS, WIDTH // 2), dtype),
        cost_estimate=pl.CostEstimate(
            flops=2 * ROWS * WIDTH * WIDTH, bytes_accessed=11 << 20, transcendentals=0
        ),
        name="back",
    )(half, du_f, du_r, weight, weight)


def shards(hidden, in_weight, state_proj, log_decay, step_size, skip_gain, cotangent):
    table = jnp.concatenate([log_decay[0], log_decay[1], step_size[0], step_size[1]], axis=1)
    gains = jnp.broadcast_to(jnp.tile(skip_gain, 4)[None], (8, TILE))
    pack = jnp.concatenate([table, gains], axis=0)
    other_pack = chan_swap(pack)
    other_cot = chan_swap(cotangent)
    u_f, u_r, states = project(hidden, in_weight, state_proj, pack, cotangent)
    keep, send = whole(
        mirror_kernel,
        [shape(SLICES // 2, FULL, TILE)] * 2,
        (cotangent, state_proj, pack, other_pack, states),
        name="mirror",
    )
    other_u = chan_swap(u_r)
    f_carry, b_carry, r_carry = carries(keep, send)
    du_f, du_r = grads(cotangent, other_cot, state_proj, pack, f_carry, b_carry)
    here = lax.axis_index("chan").astype(jnp.int32)[None]
    given = chan_swap(back(1 - here, du_f, du_r, in_weight, BF16))
    kept = back(here, du_f, du_r, in_weight, F32)
    layer_out = layer(u_f, other_u, state_proj, pack, other_pack, f_carry, r_carry)
    input_grad = (kept + given.astype(F32)).astype(BF16)
    return (layer_out, input_grad)


def solution(mesh):
    in_specs = (
        P("ctx", None),
        P(None, "chan"),
        P(None, "ctx", None),
        P(None, "ctx", "chan"),
        P(None, "ctx", "chan"),
        P("chan"),
        P("ctx", "chan"),
    )
    out_specs = (P("ctx", "chan"), P("ctx", "chan"))
    return jax.shard_map(shards, mesh=mesh, in_specs=in_specs, out_specs=out_specs, check_vma=False)
```

```python
import jax
import jax.numpy as jnp
from jax import lax
from jax.experimental import pallas as pl
from jax.experimental.pallas import tpu as pltpu
from jax.sharding import PartitionSpec as P

F32 = jnp.float32
BF16 = jnp.bfloat16
ROWS = 256
WIDTH = 2048
LANES = 256
STEPS = WIDTH // LANES
HEAD = 64
STATE = 64
SUB = 64
TILE = 128
SLICES = WIDTH // TILE
BODY = 4 * STATE
FULL = BODY + 16
FF, RF, FB, RB = 0, 1, 2, 3
FORWARD = (True, False, False, True)
NT = (((1,), (1,)), ((), ()))


def mm(a, b):
    return jnp.dot(a, b, preferred_element_type=F32)


def mm_nt(a, b):
    return lax.dot_general(a, b, NT, preferred_element_type=F32)


def iota(shape, dim):
    return lax.broadcasted_iota(jnp.int32, shape, dim)


def split3(x):
    high = x.astype(BF16)
    rest = x - high.astype(F32)
    middle = rest.astype(BF16)
    low = (rest - middle.astype(F32)).astype(BF16)
    return high, middle, low


def exact_mm(ones, x):
    high, middle, low = split3(x)
    return mm(ones, high) + mm(ones, middle) + mm(ones, low)


def pair(x):
    high = x.astype(BF16)
    low = (x - high.astype(F32)).astype(BF16)
    return jnp.concatenate([high, low], axis=1)


def exchange_matrix(n):
    return (iota((n, n), 0) + iota((n, n), 1) == n - 1).astype(BF16)


def spread(rows, base, block, mirrored):
    row = iota((rows, LANES), 0) & 127
    head = block * (LANES // HEAD) + iota((rows, LANES), 1) // HEAD
    if mirrored:
        head = WIDTH // HEAD - 1 - head
    return (row == base + head).astype(BF16)


def picks(n, offset):
    row = iota((n, TILE), 0) & (STATE - 1)
    return (iota((n, TILE), 1) == offset + row).astype(BF16)


def place():
    index = lax.axis_index("ctx")
    return index & 1, (index >> 1) & 1, (index >> 2) & 3, index >> 4


def project_kernel(hidden, weight, proj, pack, cot, u_f, u_r, states, both, scale, keys):
    step = pl.program_id(0)

    @pl.when(step == 0)
    def _():
        flip = exchange_matrix(LANES)
        for b in range(STEPS):
            block = hidden[:, b * LANES : (b + 1) * LANES]
            back = STEPS - 1 - b
            both[0:ROWS, b * LANES : (b + 1) * LANES] = block
            both[ROWS : 2 * ROWS, back * LANES : (back + 1) * LANES] = mm(block, flip).astype(BF16)
        table = pack[0:ROWS, :]
        lane = iota((ROWS, TILE), 1)
        decay = jnp.where(lane < 64, table, 0.0)
        lower = (iota((ROWS, ROWS), 0) >= iota((ROWS, ROWS), 1)).astype(BF16)
        total = exact_mm(lower, decay)
        last = total[ROWS - 1 : ROWS, :]
        weight_of = pltpu.roll(table, 64, 1)
        values = jnp.where(
            lane < 32,
            jnp.exp(last - total) * weight_of,
            jnp.where(
                lane < 64, jnp.exp(total - decay) * weight_of, pltpu.roll(jnp.exp(total), 64, 1)
            ),
        )
        scale[...] = pair(values)
        keys[0] = mm_nt(picks(STATE, 0), proj[0]).astype(BF16)
        keys[1] = mm_nt(picks(STATE, 0), proj[1]).astype(BF16)
        keys[2] = mm_nt(picks(STATE, STATE), proj[0]).astype(BF16)

    u = mm(both[...], weight[...]).astype(BF16)
    u_f[...] = u[0:ROWS]
    u_r[...] = u[ROWS : 2 * ROWS]
    values = (u[0:ROWS].astype(F32), u[ROWS : 2 * ROWS].astype(F32), cot[...].astype(F32))
    for scan in range(3):
        wide = mm(scale[...], spread(2 * TILE, 32 * scan, step, False))
        state = mm(keys[scan], (values[scan] * wide).astype(BF16)).astype(BF16)
        for j in range(LANES // TILE):
            states[j, scan * STATE : (scan + 1) * STATE, :] = state[:, j * TILE : (j + 1) * TILE]


def project(hidden, weight, proj, pack, cot):
    columns = pl.BlockSpec((ROWS, LANES), lambda i: (0, i))
    return pl.pallas_call(
        project_kernel,
        grid=(STEPS,),
        in_specs=[
            pl.BlockSpec((ROWS, WIDTH), lambda i: (0, 0)),
            pl.BlockSpec((WIDTH, LANES), lambda i: (0, i)),
            pl.BlockSpec((2, ROWS, TILE), lambda i: (0, 0, 0)),
            pl.BlockSpec((ROWS + 8, TILE), lambda i: (0, 0)),
            columns,
        ],
        out_specs=[
            columns,
            columns,
            pl.BlockSpec((LANES // TILE, 3 * STATE, TILE), lambda i: (i, 0, 0)),
        ],
        out_shape=[
            jax.ShapeDtypeStruct((ROWS, WIDTH), BF16),
            jax.ShapeDtypeStruct((ROWS, WIDTH), BF16),
            jax.ShapeDtypeStruct((SLICES, 3 * STATE, TILE), BF16),
        ],
        scratch_shapes=[
            pltpu.VMEM((2 * ROWS, WIDTH), BF16),
            pltpu.VMEM((ROWS, 2 * TILE), BF16),
            pltpu.VMEM((3, STATE, ROWS), BF16),
        ],
        cost_estimate=pl.CostEstimate(
            flops=4 * ROWS * WIDTH * WIDTH, bytes_accessed=14 << 20, transcendentals=0
        ),
        name="project",
    )(hidden, weight, proj, pack, cot)


def mirror_kernel(cot, proj, pack, other_pack, states, keep, send):
    core, _, _, _ = place()
    decay = jnp.where(iota((ROWS, TILE), 1) < 64, other_pack[0:ROWS, :], 0.0)
    own = jnp.where(iota((ROWS, TILE), 1) < 64, pack[0:ROWS, :], 0.0)
    lower = (iota((ROWS, ROWS), 0) >= iota((ROWS, ROWS), 1)).astype(BF16)
    total = exact_mm(lower, decay)
    last = total[ROWS - 1 : ROWS, :]
    scale = pair(jnp.exp(last - total + decay))
    keys = mm_nt(picks(STATE, STATE), proj[1]).astype(BF16)
    own_last = exact_mm(jnp.ones((16, ROWS), BF16), own)
    other_last = jnp.broadcast_to(last, (16, TILE))
    row, lane = iota((16, TILE), 0), iota((16, TILE), 1)
    scan, part = row // 3, row % 3

    def parts(x, wanted):
        high, middle, low = split3(jnp.exp(x))
        chosen = jnp.where(
            part == 0, high.astype(F32), jnp.where(part == 1, middle.astype(F32), low.astype(F32))
        )
        return jnp.where(wanted, chosen, 0.0).astype(BF16)

    direction = lane // 32
    own_rows = parts(own_last, (scan < 3) & (direction == (scan == RF).astype(jnp.int32)))
    other_rows = parts(other_last, (scan == RB) & (direction == 1))
    head_row = iota((TILE, LANES), 0) & 31
    for b in range(STEPS):
        head = b * (LANES // HEAD) + iota((TILE, LANES), 1) // HEAD
        straight = (head_row == head).astype(BF16)
        turned = (head_row == WIDTH // HEAD - 1 - head).astype(BF16)
        decays = (mm(own_rows, straight) + mm(other_rows, turned)).astype(BF16)
        wide = mm(scale, spread(2 * TILE, 32, b, True))
        block = cot[:, b * LANES : (b + 1) * LANES].astype(F32)
        state = mm(keys, (block * wide).astype(BF16)).astype(BF16)
        for j in range(LANES // TILE):
            s = b * (LANES // TILE) + j
            half, at = s // (SLICES // 2), s % (SLICES // 2)
            columns = slice(j * TILE, (j + 1) * TILE)

            def write(out):
                out[at, 0 : 3 * STATE, :] = states[s]
                out[at, 3 * STATE : BODY, :] = state[:, columns]
                out[at, BODY:FULL, :] = decays[:, columns]

            @pl.when(core == half)
            def _():
                write(keep)

            @pl.when(core != half)
            def _():
                write(send)


def whole(kernel, outs, args, scratch=(), name=None, flops=0, after=(), through=()):
    bytes_accessed = sum(a.size * a.dtype.itemsize for a in args)
    bytes_accessed += sum(2 * o.size for o in outs)
    first = len(args)
    start = first + len(after) + len(through)
    end = start + len(outs)

    def body(*refs):
        kernel(*refs[:first], *refs[start:end], *refs[end + len(through) :])

    there = [pl.BlockSpec(memory_space=pl.ANY)]
    return pl.pallas_call(
        body,
        out_shape=list(outs) + [jax.ShapeDtypeStruct(t.shape, t.dtype) for t in through],
        in_specs=[pl.BlockSpec(memory_space=pltpu.VMEM)] * len(args)
        + there * (len(after) + len(through)),
        out_specs=[pl.BlockSpec(memory_space=pltpu.VMEM)] * len(outs) + there * len(through),
        input_output_aliases={first + len(after) + i: len(outs) + i for i in range(len(through))},
        scratch_shapes=list(scratch),
        cost_estimate=pl.CostEstimate(
            flops=flops, bytes_accessed=bytes_accessed, transcendentals=0
        ),
        name=name,
    )(*args, *after, *through)


def shape(*dims):
    return jax.ShapeDtypeStruct(dims, BF16)


def read_decays(tile):
    tile = tile.astype(F32)
    return [
        tile[3 * i : 3 * i + 1] + tile[3 * i + 1 : 3 * i + 2] + tile[3 * i + 2 : 3 * i + 3]
        for i in range(tile.shape[0] // 4)
    ]


def decay_rows(decays):
    row = iota((16, TILE), 0)
    out = jnp.zeros((16, TILE), F32)
    for i, d in enumerate(decays):
        for j, p in enumerate(split3(d)):
            out = jnp.where(row == 3 * i + j, p.astype(F32), out)
    return out.astype(BF16)


def rows_of(scan):
    return slice(scan * STATE, (scan + 1) * STATE)


def pair_total(own, got, at, first, out, to):
    mine, theirs = read_decays(own[at, BODY:FULL, :]), read_decays(got[at, BODY:FULL, :])
    for scan in range(4):
        early = first if FORWARD[scan] else 1.0 - first
        alpha = early * theirs[scan] + (1.0 - early)
        beta = early + (1.0 - early) * mine[scan]
        out[to, rows_of(scan), :] = (
            alpha * own[at, rows_of(scan), :].astype(F32)
            + beta * got[at, rows_of(scan), :].astype(F32)
        ).astype(BF16)
    out[to, BODY:FULL, :] = decay_rows([a * b for a, b in zip(mine, theirs)])


def pair_carry(own, got, at, first, carry, mine, theirs, scan):
    early = first if FORWARD[scan] else 1.0 - first
    here = (1.0 - early) * (theirs[scan] * carry + got[at, rows_of(scan), :].astype(F32))
    here = here + early * carry
    there = early * (mine[scan] * carry + own[at, rows_of(scan), :].astype(F32))
    there = there + (1.0 - early) * carry
    return here.astype(BF16), there.astype(BF16)


def core_up_kernel(own, got, keep, send):
    core, x, _, _ = place()
    first = 1.0 - core.astype(F32)

    @pl.loop(0, 4)
    def _(j):
        pair_total(own, got, x * 4 + j, first, keep, j)
        pair_total(own, got, (1 - x) * 4 + j, first, send, j)


def x_up_kernel(own, got, *outs):
    _, x, y, _ = place()
    first = 1.0 - x.astype(F32)
    for k in range(4):
        pair_total(own, got, (y + k) & 3, first, outs[k], 0)


def y_total_kernel(a0, a1, a2, a3, z1, z2, z3, stack, total):
    _, _, y, z = place()
    for k, a in enumerate((a0, a1, a2, a3)):
        stack[(y - k) & 3] = a[0]
    decays = [read_decays(stack[p, BODY:FULL, :]) for p in range(4)]
    for scan in range(4):
        order = (0, 1, 2, 3) if FORWARD[scan] else (3, 2, 1, 0)
        t = stack[order[0], rows_of(scan), :].astype(F32)
        for p in order[1:]:
            t = decays[p][scan] * t + stack[p, rows_of(scan), :].astype(F32)
        total[rows_of(scan), :] = t.astype(BF16)
    product = [decays[0][s] * decays[1][s] * decays[2][s] * decays[3][s] for s in range(4)]
    later = decay_rows([product[FF], product[RB]])
    earlier = decay_rows([product[RF], product[FB]])
    for k, out in enumerate((z1, z2, z3)):

        @pl.when(z + k + 1 < 4)
        def _():
            out[0:STATE, :] = total[rows_of(FF), :]
            out[STATE : 2 * STATE, :] = total[rows_of(RB), :]
            out[2 * STATE :, :] = later

        @pl.when(z + k + 1 >= 4)
        def _():
            out[0:STATE, :] = total[rows_of(RF), :]
            out[STATE : 2 * STATE, :] = total[rows_of(FB), :]
            out[2 * STATE :, :] = earlier


def z_carry_kernel(a0, a1, a2, a3, q1, q2, q3, d0, d1, d2, d3, stack, out):
    _, _, y, z = place()
    for k, a in enumerate((a0, a1, a2, a3)):
        stack[(y - k) & 3] = a[0]
    decays = [read_decays(stack[p, BODY:FULL, :]) for p in range(4)]
    got = (q1, q2, q3)
    plane = [read_decays(q[2 * STATE :, :]) for q in got]
    before = [(z >= k).astype(F32) for k in (1, 2, 3)]
    for scan in range(4):
        half = 0 if scan in (FF, RF) else 1
        part = [q[half * STATE : (half + 1) * STATE, :].astype(F32) for q in got]
        d = [p[half] for p in plane]
        if FORWARD[scan]:
            m = before
            order, positions = (0, 1, 2), (0, 1, 2, 3)
        else:
            m = [1.0 - b for b in before]
            order, positions = (2, 1, 0), (3, 2, 1, 0)
        i, j, k = order
        c = m[i] * (part[i] + d[i] * (m[j] * (part[j] + d[j] * (m[k] * part[k]))))
        for p in positions:
            out[p, rows_of(scan), :] = c.astype(BF16)
            if p != positions[-1]:
                c = decays[p][scan] * c + stack[p, rows_of(scan), :].astype(F32)
    for k, d in enumerate((d0, d1, d2, d3)):
        d[...] = out[(y - k) & 3]


def x_down_kernel(c0, c1, c2, c3, own, got, keep, send):
    _, x, y, _ = place()
    first = 1.0 - x.astype(F32)
    for k, c in enumerate((c0, c1, c2, c3)):
        at = (y + k) & 3
        mine, theirs = read_decays(own[at, BODY:FULL, :]), read_decays(got[at, BODY:FULL, :])
        for scan in range(4):
            here, there = pair_carry(
                own, got, at, first, c[rows_of(scan), :].astype(F32), mine, theirs, scan
            )
            keep[at, rows_of(scan), :] = here
            send[at, rows_of(scan), :] = there


def core_down_kernel(c_own, c_got, own, got, f_keep, f_send, b_same, b_cross, r_same, r_cross):
    core, x, _, _ = place()
    first = 1.0 - core.astype(F32)

    @pl.loop(0, 4)
    def _(j):
        for carry, side in ((c_own, x), (c_got, 1 - x)):
            at = side * 4 + j
            mine, theirs = read_decays(own[at, BODY:FULL, :]), read_decays(got[at, BODY:FULL, :])
            for scan, here_out, there_out, row in (
                (FF, f_keep, f_send, 0),
                (FB, f_keep, f_send, STATE),
                (RB, b_same, b_cross, 0),
                (RF, r_same, r_cross, 0),
            ):
                here, there = pair_carry(
                    own,
                    got,
                    at,
                    first,
                    carry[j, rows_of(scan), :].astype(F32),
                    mine,
                    theirs,
                    scan,
                )
                here_out[at, row : row + STATE, :] = here
                there_out[at, row : row + STATE, :] = there


def ctx_permute(x, target):
    return lax.ppermute(x, "ctx", [(i, target(i)) for i in range(64)])


def core_swap(x):
    return ctx_permute(x, lambda i: i ^ 1)


def x_swap(x):
    return ctx_permute(x, lambda i: i ^ 2)


def y_shift(x, k):
    return ctx_permute(x, lambda i: (i & ~12) | ((i + 4 * k) & 12))


def z_shift(x, k):
    return ctx_permute(x, lambda i: (i + 16 * k) & 63)


def chan_swap(x):
    return lax.ppermute(x, "chan", [(0, 1), (1, 0)])


def cross_swap(x):
    return lax.ppermute(x, ("ctx", "chan"), [(i, i ^ 3) for i in range(128)])


def carries(keep1, send1, other_cot, u_r):
    slices = SLICES // 2
    got1 = core_swap(send1)
    keep2, send2 = whole(
        core_up_kernel,
        [shape(4, FULL, TILE)] * 2,
        (keep1, got1),
        name="core_up",
        after=(other_cot,),
    )
    got2 = x_swap(send2)
    *tops, u_r = whole(
        x_up_kernel, [shape(1, FULL, TILE)] * 4, (keep2, got2), name="x_up", through=(u_r,)
    )
    other_u = chan_swap(u_r)
    row = [tops[0]] + [y_shift(tops[k], k) for k in (1, 2, 3)]
    stack = pltpu.VMEM((4, FULL, TILE), BF16)
    planes = whole(
        y_total_kernel,
        [shape(2 * STATE + 16, TILE)] * 3,
        row,
        [stack, pltpu.VMEM((BODY, TILE), BF16)],
        name="y_total",
    )
    other = [z_shift(planes[k - 1], k) for k in (1, 2, 3)]
    down = whole(
        z_carry_kernel,
        [shape(BODY, TILE)] * 4,
        row + other,
        [stack, pltpu.VMEM((4, BODY, TILE), BF16)],
        name="z_carry",
    )
    down = [down[0]] + [y_shift(down[k], -k) for k in (1, 2, 3)]
    keep3, send3 = whole(
        x_down_kernel,
        [shape(4, BODY, TILE)] * 2,
        [*down, keep2, got2],
        name="x_down",
        after=(other_u,),
    )
    got3 = x_swap(send3)
    f_keep, f_send, b_same, b_cross, r_same, r_cross = whole(
        core_down_kernel,
        [shape(slices, 2 * STATE, TILE)] * 2 + [shape(slices, STATE, TILE)] * 4,
        (keep3, got3, keep1, got1),
        name="core_down",
    )
    return (
        other_u,
        (f_keep, core_swap(f_send)),
        (chan_swap(b_same), cross_swap(b_cross)),
        (chan_swap(r_same), cross_swap(r_cross)),
    )


def prepare(tables, proj_of, forward, exclusive, with_weight, in_scale, out_scale, rows_scale):
    lane = iota((ROWS, TILE), 1)
    first, second = tables
    table = jnp.where(lane & 32 == 0, first[0:ROWS, :], second[0:ROWS, :])
    decay = jnp.where(lane < 64, table, 0.0)
    weight = pltpu.roll(table, 64, 1)
    row, column = iota((ROWS, ROWS), 0), iota((ROWS, ROWS), 1)
    same = row // SUB == column // SUB
    total = exact_mm((same & (row >= column)).astype(BF16), decay)
    full = exact_mm(same.astype(BF16), decay)

    def level(i):
        c = total if forward[i] else full - total + decay
        return c - decay if exclusive[i] else c

    rise = jnp.where(lane < 32, level(0), level(1)) - 0.5 * full
    in_scale[...] = pair(jnp.exp(-rise) * weight if with_weight else jnp.exp(-rise))
    out_scale[...] = pair(jnp.exp(rise) if with_weight else jnp.exp(rise) * weight)
    small = iota((16, TILE), 0)
    tail = jnp.where(
        iota((8, TILE), 1) & 32 == 0, first[ROWS : ROWS + 8, :], second[ROWS : ROWS + 8, :]
    )
    half = jnp.exp(0.5 * full)
    values = jnp.broadcast_to(tail[0:1], (16, TILE))
    for b in range(ROWS // SUB):
        values = jnp.where(small == b, half[b * SUB : b * SUB + 1], values)
    rows_scale[...] = pair(values)


def prepare_matrices(proj, query_at, forward, inside, query, keys):
    key_at = STATE - query_at
    row, column = iota((ROWS, ROWS), 0), iota((ROWS, ROWS), 1)
    same = row // SUB == column // SUB
    order = (row >= column) if forward else (row <= column)
    tiled_query = mm_nt(proj, picks(ROWS, query_at))
    tiled_keys = mm_nt(picks(ROWS, key_at), proj)
    q = jnp.where(iota((ROWS, TILE), 1) // STATE == query_at // STATE, proj.astype(F32), 0.0)
    swapped = pltpu.roll(proj.astype(F32), STATE, 1).astype(BF16)
    affinity = mm_nt(q.astype(BF16), swapped)
    inside[...] = jnp.where(same & order, affinity, 0.0).astype(BF16)
    query[...] = jnp.where(same, tiled_query, 0.0).astype(BF16)
    keys[...] = jnp.where(same, tiled_keys, 0.0).astype(BF16)


def scan_block(values, carry, forward, lanes, in_scale, out_scale, rows_scale, mats):
    inside, query, keys = mats
    wide = mm(in_scale[...], lanes)
    small = mm(rows_scale[...], lanes)
    out = mm(out_scale[...], lanes)
    scaled = (values * wide).astype(BF16)
    fresh = mm(keys[...], scaled)
    blocks = ROWS // SUB
    entering = [None] * blocks
    state = carry
    for b in range(blocks) if forward else range(blocks - 1, -1, -1):
        half = small[b : b + 1]
        met = half * state
        entering[b] = met.astype(BF16)
        state = half * (met + fresh[b * SUB : (b + 1) * SUB])
    scan = mm(inside[...], scaled) + mm(query[...], jnp.concatenate(entering, axis=0))
    return scan * out + small[8:9] * values


def carry_block(keep, got, core, block, row):
    mine = (core == block // (STEPS // 2)).astype(F32)
    parts = [
        mine * keep[j, row : row + STATE, :].astype(F32)
        + (1.0 - mine) * got[j, row : row + STATE, :].astype(F32)
        for j in range(LANES // TILE)
    ]
    return jnp.concatenate(parts, axis=1)


def grads_kernel(
    cot, other_cot, proj, pack, f_keep, f_got, b_keep, b_got, du_f, du_r, *scratch
):
    step = pl.program_id(0)
    core, _, _, _ = place()
    in_scale, out_scale, rows_scale = scratch[0:3]
    straight, turned = scratch[3:6], scratch[6:9]

    @pl.when(step == 0)
    def _():
        tables = (pack, pack)
        prepare(
            tables, proj, (False, True), (True, True), False, in_scale, out_scale, rows_scale
        )
        prepare_matrices(proj[0], 0, False, *straight)
        prepare_matrices(proj[1], 0, True, *turned)

    back = STEPS - 1 - step
    du_f[...] = scan_block(
        cot[...].astype(F32),
        carry_block(f_keep, f_got, core, step, STATE),
        False,
        spread(2 * TILE, 0, step, False),
        in_scale,
        out_scale,
        rows_scale,
        straight,
    ).astype(BF16)
    mirrored = scan_block(
        other_cot[...].astype(F32),
        carry_block(b_keep, b_got, core, back, 0),
        True,
        spread(2 * TILE, 32, back, True),
        in_scale,
        out_scale,
        rows_scale,
        turned,
    ).astype(BF16)
    du_r[...] = mm(mirrored, exchange_matrix(LANES)).astype(BF16)


def layer_kernel(
    u_f, other_u, proj, pack, other_pack, f_keep, f_got, r_keep, r_got, out, *scratch
):
    step = pl.program_id(0)
    core, _, _, _ = place()
    in_scale, out_scale, rows_scale = scratch[0:3]
    straight, turned = scratch[3:6], scratch[6:9]

    @pl.when(step == 0)
    def _():
        tables = (pack, other_pack)
        prepare(
            tables, proj, (True, False), (False, False), True, in_scale, out_scale, rows_scale
        )
        prepare_matrices(proj[0], STATE, True, *straight)
        prepare_matrices(proj[1], STATE, False, *turned)

    back = STEPS - 1 - step
    y_f = scan_block(
        u_f[...].astype(F32),
        carry_block(f_keep, f_got, core, step, 0),
        True,
        spread(2 * TILE, 0, step, False),
        in_scale,
        out_scale,
        rows_scale,
        straight,
    )
    y_r = scan_block(
        other_u[...].astype(F32),
        carry_block(r_keep, r_got, core, back, 0),
        False,
        spread(2 * TILE, 32, back, False),
        in_scale,
        out_scale,
        rows_scale,
        turned,
    ).astype(BF16)
    out[...] = (y_f + mm(y_r, exchange_matrix(LANES))).astype(BF16)


def scan_scratch():
    square = pltpu.VMEM((ROWS, ROWS), BF16)
    wide = pltpu.VMEM((ROWS, 2 * TILE), BF16)
    return [wide, wide, pltpu.VMEM((16, 2 * TILE), BF16)] + [square] * 6


def carry_specs(rows, mirrored):
    half = STEPS // 2
    if mirrored:
        return [pl.BlockSpec((LANES // TILE, rows, TILE), lambda i: ((STEPS - 1 - i) % half, 0, 0))] * 2
    return [pl.BlockSpec((LANES // TILE, rows, TILE), lambda i: (i % half, 0, 0))] * 2


COLUMNS = pl.BlockSpec((ROWS, LANES), lambda i: (0, i))
MIRRORED = pl.BlockSpec((ROWS, LANES), lambda i: (0, STEPS - 1 - i))
PROJ = pl.BlockSpec((2, ROWS, TILE), lambda i: (0, 0, 0))
PACK = pl.BlockSpec((ROWS + 8, TILE), lambda i: (0, 0))
SCAN_COST = pl.CostEstimate(flops=10 << 30, bytes_accessed=6 << 20, transcendentals=0)


def grads(cot, other_cot, proj, pack, f_carry, b_carry):
    return pl.pallas_call(
        grads_kernel,
        grid=(STEPS,),
        in_specs=[COLUMNS, MIRRORED, PROJ, PACK]
        + carry_specs(2 * STATE, False)
        + carry_specs(STATE, True),
        out_specs=[COLUMNS, COLUMNS],
        out_shape=[shape(ROWS, WIDTH), shape(ROWS, WIDTH)],
        scratch_shapes=scan_scratch(),
        cost_estimate=SCAN_COST,
        name="grads",
    )(cot, other_cot, proj, pack, *f_carry, *b_carry)


def layer(u_f, other_u, proj, pack, other_pack, f_carry, r_carry):
    return pl.pallas_call(
        layer_kernel,
        grid=(STEPS,),
        in_specs=[COLUMNS, MIRRORED, PROJ, PACK, PACK]
        + carry_specs(2 * STATE, False)
        + carry_specs(STATE, True),
        out_specs=COLUMNS,
        out_shape=shape(ROWS, WIDTH),
        scratch_shapes=scan_scratch(),
        cost_estimate=SCAN_COST,
        name="layer",
    )(u_f, other_u, proj, pack, other_pack, *f_carry, *r_carry)


def back_kernel(half, du_f, du_r, direct, mirrored, *rest):
    total = mm_nt(du_f[...], direct[...])
    turn = mm_nt(du_r[...], mirrored[...])
    high = turn.astype(BF16)
    low = (turn - high.astype(F32)).astype(BF16)
    flip = exchange_matrix(LANES)
    total = total + mm(high, flip) + mm(low, flip)
    if len(rest) == 2:
        total = total + rest[0][...].astype(F32)
    rest[-1][...] = total.astype(rest[-1].dtype)


def back(half, du_f, du_r, weight, dtype):
    steps = STEPS // 2
    spec = pltpu.PrefetchScalarGridSpec(
        num_scalar_prefetch=1,
        grid=(steps,),
        in_specs=[
            pl.BlockSpec((ROWS, WIDTH), lambda i, h: (0, 0)),
            pl.BlockSpec((ROWS, WIDTH), lambda i, h: (0, 0)),
            pl.BlockSpec((LANES, WIDTH), lambda i, h: (h[0] * steps + i, 0)),
            pl.BlockSpec((LANES, WIDTH), lambda i, h: (STEPS - 1 - h[0] * steps - i, 0)),
        ],
        out_specs=pl.BlockSpec((ROWS, LANES), lambda i, h: (0, i)),
    )
    return pl.pallas_call(
        back_kernel,
        grid_spec=spec,
        out_shape=jax.ShapeDtypeStruct((ROWS, WIDTH // 2), dtype),
        cost_estimate=pl.CostEstimate(
            flops=2 * ROWS * WIDTH * WIDTH, bytes_accessed=11 << 20, transcendentals=0
        ),
        name="back",
    )(half, du_f, du_r, weight, weight)


def shards(hidden, in_weight, state_proj, log_decay, step_size, skip_gain, cotangent):
    table = jnp.concatenate([log_decay[0], log_decay[1], step_size[0], step_size[1]], axis=1)
    gains = jnp.broadcast_to(jnp.tile(skip_gain, 4)[None], (8, TILE))
    pack = jnp.concatenate([table, gains], axis=0)
    other_pack = chan_swap(pack)
    other_cot = chan_swap(cotangent)
    u_f, u_r, states = project(hidden, in_weight, state_proj, pack, cotangent)
    keep, send = whole(
        mirror_kernel,
        [shape(SLICES // 2, FULL, TILE)] * 2,
        (cotangent, state_proj, pack, other_pack, states),
        name="mirror",
    )
    other_u, f_carry, b_carry, r_carry = carries(keep, send, other_cot, u_r)
    du_f, du_r = grads(cotangent, other_cot, state_proj, pack, f_carry, b_carry)
    here = lax.axis_index("chan").astype(jnp.int32)[None]
    given = chan_swap(back(1 - here, du_f, du_r, in_weight, BF16))
    kept = back(here, du_f, du_r, in_weight, F32)
    layer_out = layer(u_f, other_u, state_proj, pack, other_pack, f_carry, r_carry)
    input_grad = (kept + given.astype(F32)).astype(BF16)
    return (layer_out, input_grad)


def solution(mesh):
    in_specs = (
        P("ctx", None),
        P(None, "chan"),
        P(None, "ctx", None),
        P(None, "ctx", "chan"),
        P(None, "ctx", "chan"),
        P("chan"),
        P("ctx", "chan"),
    )
    out_specs = (P("ctx", "chan"), P("ctx", "chan"))
    return jax.shard_map(shards, mesh=mesh, in_specs=in_specs, out_specs=out_specs, check_vma=False)
```

```python
import jax
import jax.numpy as jnp
from jax import lax
from jax.experimental import pallas as pl
from jax.experimental.pallas import tpu as pltpu
from jax.sharding import PartitionSpec as P

F32 = jnp.float32
BF16 = jnp.bfloat16
ROWS = 256
WIDTH = 2048
LANES = 256
STEPS = WIDTH // LANES
HEAD = 64
STATE = 64
SUB = 64
TILE = 128
SLICES = WIDTH // TILE
BODY = 4 * STATE
FULL = BODY + 16
FF, RF, FB, RB = 0, 1, 2, 3
FORWARD = (True, False, False, True)
NT = (((1,), (1,)), ((), ()))


def mm(a, b):
    return jnp.dot(a, b, preferred_element_type=F32)


def mm_nt(a, b):
    return lax.dot_general(a, b, NT, preferred_element_type=F32)


def iota(shape, dim):
    return lax.broadcasted_iota(jnp.int32, shape, dim)


def split3(x):
    high = x.astype(BF16)
    rest = x - high.astype(F32)
    middle = rest.astype(BF16)
    low = (rest - middle.astype(F32)).astype(BF16)
    return high, middle, low


def exact_mm(ones, x):
    high, middle, low = split3(x)
    return mm(ones, high) + mm(ones, middle) + mm(ones, low)


def pair(x):
    high = x.astype(BF16)
    low = (x - high.astype(F32)).astype(BF16)
    return jnp.concatenate([high, low], axis=1)


def exchange_matrix(n):
    return (iota((n, n), 0) + iota((n, n), 1) == n - 1).astype(BF16)


def spread(rows, base, block, mirrored):
    row = iota((rows, LANES), 0) & 127
    head = block * (LANES // HEAD) + iota((rows, LANES), 1) // HEAD
    if mirrored:
        head = WIDTH // HEAD - 1 - head
    return (row == base + head).astype(BF16)


def picks(n, offset):
    row = iota((n, TILE), 0) & (STATE - 1)
    return (iota((n, TILE), 1) == offset + row).astype(BF16)


def place():
    index = lax.axis_index("ctx")
    return index & 1, (index >> 1) & 1, (index >> 2) & 3, index >> 4


def project_kernel(hidden, weight, proj, pack, cot, u_f, u_r, states, both, scale, keys):
    step = pl.program_id(0)

    @pl.when(step == 0)
    def _():
        flip = exchange_matrix(LANES)
        for b in range(STEPS):
            block = hidden[:, b * LANES : (b + 1) * LANES]
            back = STEPS - 1 - b
            both[0:ROWS, b * LANES : (b + 1) * LANES] = block
            both[ROWS : 2 * ROWS, back * LANES : (back + 1) * LANES] = mm(block, flip).astype(BF16)
        table = pack[0:ROWS, :]
        lane = iota((ROWS, TILE), 1)
        decay = jnp.where(lane < 64, table, 0.0)
        lower = (iota((ROWS, ROWS), 0) >= iota((ROWS, ROWS), 1)).astype(BF16)
        total = exact_mm(lower, decay)
        last = total[ROWS - 1 : ROWS, :]
        weight_of = pltpu.roll(table, 64, 1)
        values = jnp.where(
            lane < 32,
            jnp.exp(last - total) * weight_of,
            jnp.where(
                lane < 64, jnp.exp(total - decay) * weight_of, pltpu.roll(jnp.exp(total), 64, 1)
            ),
        )
        scale[...] = pair(values)
        keys[0] = mm_nt(picks(STATE, 0), proj[0]).astype(BF16)
        keys[1] = mm_nt(picks(STATE, 0), proj[1]).astype(BF16)
        keys[2] = mm_nt(picks(STATE, STATE), proj[0]).astype(BF16)

    u = mm(both[...], weight[...]).astype(BF16)
    u_f[...] = u[0:ROWS]
    u_r[...] = u[ROWS : 2 * ROWS]
    values = (u[0:ROWS].astype(F32), u[ROWS : 2 * ROWS].astype(F32), cot[...].astype(F32))
    for scan in range(3):
        wide = mm(scale[...], spread(2 * TILE, 32 * scan, step, False))
        state = mm(keys[scan], (values[scan] * wide).astype(BF16)).astype(BF16)
        for j in range(LANES // TILE):
            states[j, scan * STATE : (scan + 1) * STATE, :] = state[:, j * TILE : (j + 1) * TILE]


def project(hidden, weight, proj, pack, cot):
    columns = pl.BlockSpec((ROWS, LANES), lambda i: (0, i))
    return pl.pallas_call(
        project_kernel,
        grid=(STEPS,),
        in_specs=[
            pl.BlockSpec((ROWS, WIDTH), lambda i: (0, 0)),
            pl.BlockSpec((WIDTH, LANES), lambda i: (0, i)),
            pl.BlockSpec((2, ROWS, TILE), lambda i: (0, 0, 0)),
            pl.BlockSpec((ROWS + 8, TILE), lambda i: (0, 0)),
            columns,
        ],
        out_specs=[
            columns,
            columns,
            pl.BlockSpec((LANES // TILE, 3 * STATE, TILE), lambda i: (i, 0, 0)),
        ],
        out_shape=[
            jax.ShapeDtypeStruct((ROWS, WIDTH), BF16),
            jax.ShapeDtypeStruct((ROWS, WIDTH), BF16),
            jax.ShapeDtypeStruct((SLICES, 3 * STATE, TILE), BF16),
        ],
        scratch_shapes=[
            pltpu.VMEM((2 * ROWS, WIDTH), BF16),
            pltpu.VMEM((ROWS, 2 * TILE), BF16),
            pltpu.VMEM((3, STATE, ROWS), BF16),
        ],
        cost_estimate=pl.CostEstimate(
            flops=4 * ROWS * WIDTH * WIDTH, bytes_accessed=14 << 20, transcendentals=0
        ),
        name="project",
    )(hidden, weight, proj, pack, cot)


def mirror_kernel(cot, proj, pack, other_pack, states, keep, send):
    core, _, _, _ = place()
    decay = jnp.where(iota((ROWS, TILE), 1) < 64, other_pack[0:ROWS, :], 0.0)
    own = jnp.where(iota((ROWS, TILE), 1) < 64, pack[0:ROWS, :], 0.0)
    lower = (iota((ROWS, ROWS), 0) >= iota((ROWS, ROWS), 1)).astype(BF16)
    total = exact_mm(lower, decay)
    last = total[ROWS - 1 : ROWS, :]
    scale = pair(jnp.exp(last - total + decay))
    keys = mm_nt(picks(STATE, STATE), proj[1]).astype(BF16)
    own_last = exact_mm(jnp.ones((16, ROWS), BF16), own)
    other_last = jnp.broadcast_to(last, (16, TILE))
    row, lane = iota((16, TILE), 0), iota((16, TILE), 1)
    scan, part = row // 3, row % 3

    def parts(x, wanted):
        high, middle, low = split3(jnp.exp(x))
        chosen = jnp.where(
            part == 0, high.astype(F32), jnp.where(part == 1, middle.astype(F32), low.astype(F32))
        )
        return jnp.where(wanted, chosen, 0.0).astype(BF16)

    direction = lane // 32
    own_rows = parts(own_last, (scan < 3) & (direction == (scan == RF).astype(jnp.int32)))
    other_rows = parts(other_last, (scan == RB) & (direction == 1))
    head_row = iota((TILE, LANES), 0) & 31
    for b in range(STEPS):
        head = b * (LANES // HEAD) + iota((TILE, LANES), 1) // HEAD
        straight = (head_row == head).astype(BF16)
        turned = (head_row == WIDTH // HEAD - 1 - head).astype(BF16)
        decays = (mm(own_rows, straight) + mm(other_rows, turned)).astype(BF16)
        wide = mm(scale, spread(2 * TILE, 32, b, True))
        block = cot[:, b * LANES : (b + 1) * LANES].astype(F32)
        state = mm(keys, (block * wide).astype(BF16)).astype(BF16)
        for j in range(LANES // TILE):
            s = b * (LANES // TILE) + j
            half, at = s // (SLICES // 2), s % (SLICES // 2)
            columns = slice(j * TILE, (j + 1) * TILE)

            def write(out):
                out[at, 0 : 3 * STATE, :] = states[s]
                out[at, 3 * STATE : BODY, :] = state[:, columns]
                out[at, BODY:FULL, :] = decays[:, columns]

            @pl.when(core == half)
            def _():
                write(keep)

            @pl.when(core != half)
            def _():
                write(send)


def whole(kernel, outs, args, scratch=(), name=None, flops=0, after=(), through=()):
    bytes_accessed = sum(a.size * a.dtype.itemsize for a in args)
    bytes_accessed += sum(2 * o.size for o in outs)
    first = len(args)
    start = first + len(after) + len(through)
    end = start + len(outs)

    def body(*refs):
        kernel(*refs[:first], *refs[start:end], *refs[end + len(through) :])

    there = [pl.BlockSpec(memory_space=pl.ANY)]
    return pl.pallas_call(
        body,
        out_shape=list(outs) + [jax.ShapeDtypeStruct(t.shape, t.dtype) for t in through],
        in_specs=[pl.BlockSpec(memory_space=pltpu.VMEM)] * len(args)
        + there * (len(after) + len(through)),
        out_specs=[pl.BlockSpec(memory_space=pltpu.VMEM)] * len(outs) + there * len(through),
        input_output_aliases={first + len(after) + i: len(outs) + i for i in range(len(through))},
        scratch_shapes=list(scratch),
        cost_estimate=pl.CostEstimate(
            flops=flops, bytes_accessed=bytes_accessed, transcendentals=0
        ),
        name=name,
    )(*args, *after, *through)


def shape(*dims):
    return jax.ShapeDtypeStruct(dims, BF16)


def read_decays(tile):
    tile = tile.astype(F32)
    return [
        tile[3 * i : 3 * i + 1] + tile[3 * i + 1 : 3 * i + 2] + tile[3 * i + 2 : 3 * i + 3]
        for i in range(tile.shape[0] // 4)
    ]


def decay_rows(decays):
    row = iota((16, TILE), 0)
    out = jnp.zeros((16, TILE), F32)
    for i, d in enumerate(decays):
        for j, p in enumerate(split3(d)):
            out = jnp.where(row == 3 * i + j, p.astype(F32), out)
    return out.astype(BF16)


def rows_of(scan):
    return slice(scan * STATE, (scan + 1) * STATE)


def pair_total(own, got, at, first, out, to):
    mine, theirs = read_decays(own[at, BODY:FULL, :]), read_decays(got[at, BODY:FULL, :])
    for scan in range(4):
        early = first if FORWARD[scan] else 1.0 - first
        alpha = early * theirs[scan] + (1.0 - early)
        beta = early + (1.0 - early) * mine[scan]
        out[to, rows_of(scan), :] = (
            alpha * own[at, rows_of(scan), :].astype(F32)
            + beta * got[at, rows_of(scan), :].astype(F32)
        ).astype(BF16)
    out[to, BODY:FULL, :] = decay_rows([a * b for a, b in zip(mine, theirs)])


def pair_carry(own, got, at, first, carry, mine, theirs, scan):
    early = first if FORWARD[scan] else 1.0 - first
    here = (1.0 - early) * (theirs[scan] * carry + got[at, rows_of(scan), :].astype(F32))
    here = here + early * carry
    there = early * (mine[scan] * carry + own[at, rows_of(scan), :].astype(F32))
    there = there + (1.0 - early) * carry
    return here.astype(BF16), there.astype(BF16)


def core_up_kernel(own, got, keep, send):
    core, x, _, _ = place()
    first = 1.0 - core.astype(F32)

    @pl.loop(0, 4)
    def _(j):
        pair_total(own, got, x * 4 + j, first, keep, j)
        pair_total(own, got, (1 - x) * 4 + j, first, send, j)


def x_up_kernel(own, got, *outs):
    _, x, y, _ = place()
    first = 1.0 - x.astype(F32)
    for k in range(4):
        pair_total(own, got, (y + k) & 3, first, outs[k], 0)


def y_total_kernel(a0, a1, a2, a3, z1, z2, z3, stack, total):
    _, _, y, z = place()
    for k, a in enumerate((a0, a1, a2, a3)):
        stack[(y - k) & 3] = a[0]
    decays = [read_decays(stack[p, BODY:FULL, :]) for p in range(4)]
    for scan in range(4):
        order = (0, 1, 2, 3) if FORWARD[scan] else (3, 2, 1, 0)
        t = stack[order[0], rows_of(scan), :].astype(F32)
        for p in order[1:]:
            t = decays[p][scan] * t + stack[p, rows_of(scan), :].astype(F32)
        total[rows_of(scan), :] = t.astype(BF16)
    product = [decays[0][s] * decays[1][s] * decays[2][s] * decays[3][s] for s in range(4)]
    later = decay_rows([product[FF], product[RB]])
    earlier = decay_rows([product[RF], product[FB]])
    for k, out in enumerate((z1, z2, z3)):

        @pl.when(z + k + 1 < 4)
        def _():
            out[0:STATE, :] = total[rows_of(FF), :]
            out[STATE : 2 * STATE, :] = total[rows_of(RB), :]
            out[2 * STATE :, :] = later

        @pl.when(z + k + 1 >= 4)
        def _():
            out[0:STATE, :] = total[rows_of(RF), :]
            out[STATE : 2 * STATE, :] = total[rows_of(FB), :]
            out[2 * STATE :, :] = earlier


def z_carry_kernel(a0, a1, a2, a3, q1, q2, q3, d0, d1, d2, d3, stack, out):
    _, _, y, z = place()
    for k, a in enumerate((a0, a1, a2, a3)):
        stack[(y - k) & 3] = a[0]
    decays = [read_decays(stack[p, BODY:FULL, :]) for p in range(4)]
    got = (q1, q2, q3)
    plane = [read_decays(q[2 * STATE :, :]) for q in got]
    before = [(z >= k).astype(F32) for k in (1, 2, 3)]
    for scan in range(4):
        half = 0 if scan in (FF, RF) else 1
        part = [q[half * STATE : (half + 1) * STATE, :].astype(F32) for q in got]
        d = [p[half] for p in plane]
        if FORWARD[scan]:
            m = before
            order, positions = (0, 1, 2), (0, 1, 2, 3)
        else:
            m = [1.0 - b for b in before]
            order, positions = (2, 1, 0), (3, 2, 1, 0)
        i, j, k = order
        c = m[i] * (part[i] + d[i] * (m[j] * (part[j] + d[j] * (m[k] * part[k]))))
        for p in positions:
            out[p, rows_of(scan), :] = c.astype(BF16)
            if p != positions[-1]:
                c = decays[p][scan] * c + stack[p, rows_of(scan), :].astype(F32)
    for k, d in enumerate((d0, d1, d2, d3)):
        d[...] = out[(y - k) & 3]


def x_down_kernel(c0, c1, c2, c3, own, got, keep, send):
    _, x, y, _ = place()
    first = 1.0 - x.astype(F32)
    for k, c in enumerate((c0, c1, c2, c3)):
        at = (y + k) & 3
        mine, theirs = read_decays(own[at, BODY:FULL, :]), read_decays(got[at, BODY:FULL, :])
        for scan in range(4):
            here, there = pair_carry(
                own, got, at, first, c[rows_of(scan), :].astype(F32), mine, theirs, scan
            )
            keep[at, rows_of(scan), :] = here
            send[at, rows_of(scan), :] = there


def core_down_kernel(c_own, c_got, own, got, f_keep, f_send, b_same, b_cross, r_same, r_cross):
    core, x, _, _ = place()
    first = 1.0 - core.astype(F32)

    @pl.loop(0, 4)
    def _(j):
        for carry, side in ((c_own, x), (c_got, 1 - x)):
            at = side * 4 + j
            mine, theirs = read_decays(own[at, BODY:FULL, :]), read_decays(got[at, BODY:FULL, :])
            for scan, here_out, there_out, row in (
                (FF, f_keep, f_send, 0),
                (FB, f_keep, f_send, STATE),
                (RB, b_same, b_cross, 0),
                (RF, r_same, r_cross, 0),
            ):
                here, there = pair_carry(
                    own,
                    got,
                    at,
                    first,
                    carry[j, rows_of(scan), :].astype(F32),
                    mine,
                    theirs,
                    scan,
                )
                here_out[at, row : row + STATE, :] = here
                there_out[at, row : row + STATE, :] = there


def ctx_permute(x, target):
    return lax.ppermute(x, "ctx", [(i, target(i)) for i in range(64)])


def core_swap(x):
    return ctx_permute(x, lambda i: i ^ 1)


def x_swap(x):
    return ctx_permute(x, lambda i: i ^ 2)


def y_shift(x, k):
    return ctx_permute(x, lambda i: (i & ~12) | ((i + 4 * k) & 12))


def z_shift(x, k):
    return ctx_permute(x, lambda i: (i + 16 * k) & 63)


def chan_swap(x):
    return lax.ppermute(x, "chan", [(0, 1), (1, 0)])


def cross_swap(x):
    return lax.ppermute(x, ("ctx", "chan"), [(i, i ^ 3) for i in range(128)])


def carries(keep1, send1, other_cot, u_r):
    slices = SLICES // 2
    got1 = core_swap(send1)
    keep2, send2 = whole(
        core_up_kernel,
        [shape(4, FULL, TILE)] * 2,
        (keep1, got1),
        name="core_up",
        after=(other_cot,),
    )
    got2 = x_swap(send2)
    *tops, u_r = whole(
        x_up_kernel, [shape(1, FULL, TILE)] * 4, (keep2, got2), name="x_up", through=(u_r,)
    )
    other_u = chan_swap(u_r)
    row = [tops[0]] + [y_shift(tops[k], k) for k in (1, 2, 3)]
    stack = pltpu.VMEM((4, FULL, TILE), BF16)
    planes = whole(
        y_total_kernel,
        [shape(2 * STATE + 16, TILE)] * 3,
        row,
        [stack, pltpu.VMEM((BODY, TILE), BF16)],
        name="y_total",
    )
    other = [z_shift(planes[k - 1], k) for k in (1, 2, 3)]
    down = whole(
        z_carry_kernel,
        [shape(BODY, TILE)] * 4,
        row + other,
        [stack, pltpu.VMEM((4, BODY, TILE), BF16)],
        name="z_carry",
    )
    down = [down[0]] + [y_shift(down[k], -k) for k in (1, 2, 3)]
    keep3, send3 = whole(
        x_down_kernel,
        [shape(4, BODY, TILE)] * 2,
        [*down, keep2, got2],
        name="x_down",
        after=(other_u,),
    )
    got3 = x_swap(send3)
    f_keep, f_send, b_same, b_cross, r_same, r_cross = whole(
        core_down_kernel,
        [shape(slices, 2 * STATE, TILE)] * 2 + [shape(slices, STATE, TILE)] * 4,
        (keep3, got3, keep1, got1),
        name="core_down",
    )
    return (
        other_u,
        (f_keep, core_swap(f_send)),
        (chan_swap(b_same), cross_swap(b_cross)),
        (chan_swap(r_same), cross_swap(r_cross)),
    )


def prepare(tables, proj_of, forward, exclusive, with_weight, in_scale, out_scale, rows_scale):
    lane = iota((ROWS, TILE), 1)
    first, second = tables
    table = jnp.where(lane & 32 == 0, first[0:ROWS, :], second[0:ROWS, :])
    decay = jnp.where(lane < 64, table, 0.0)
    weight = pltpu.roll(table, 64, 1)
    row, column = iota((ROWS, ROWS), 0), iota((ROWS, ROWS), 1)
    same = row // SUB == column // SUB
    total = exact_mm((same & (row >= column)).astype(BF16), decay)
    full = exact_mm(same.astype(BF16), decay)

    def level(i):
        c = total if forward[i] else full - total + decay
        return c - decay if exclusive[i] else c

    rise = jnp.where(lane < 32, level(0), level(1)) - 0.5 * full
    in_scale[...] = pair(jnp.exp(-rise) * weight if with_weight else jnp.exp(-rise))
    out_scale[...] = pair(jnp.exp(rise) if with_weight else jnp.exp(rise) * weight)
    small = iota((16, TILE), 0)
    tail = jnp.where(
        iota((8, TILE), 1) & 32 == 0, first[ROWS : ROWS + 8, :], second[ROWS : ROWS + 8, :]
    )
    half = jnp.exp(0.5 * full)
    values = jnp.broadcast_to(tail[0:1], (16, TILE))
    for b in range(ROWS // SUB):
        values = jnp.where(small == b, half[b * SUB : b * SUB + 1], values)
    rows_scale[...] = pair(values)


def prepare_matrices(proj, query_at, forward, inside, query, keys):
    key_at = STATE - query_at
    row, column = iota((ROWS, ROWS), 0), iota((ROWS, ROWS), 1)
    same = row // SUB == column // SUB
    order = (row >= column) if forward else (row <= column)
    tiled_query = mm_nt(proj, picks(ROWS, query_at))
    tiled_keys = mm_nt(picks(ROWS, key_at), proj)
    q = jnp.where(iota((ROWS, TILE), 1) // STATE == query_at // STATE, proj.astype(F32), 0.0)
    swapped = pltpu.roll(proj.astype(F32), STATE, 1).astype(BF16)
    affinity = mm_nt(q.astype(BF16), swapped)
    inside[...] = jnp.where(same & order, affinity, 0.0).astype(BF16)
    query[...] = jnp.where(same, tiled_query, 0.0).astype(BF16)
    keys[...] = jnp.where(same, tiled_keys, 0.0).astype(BF16)


def scan_block(values, carry, forward, lanes, in_scale, out_scale, rows_scale, mats):
    inside, query, keys = mats
    wide = mm(in_scale[...], lanes)
    small = mm(rows_scale[...], lanes)
    out = mm(out_scale[...], lanes)
    scaled = (values * wide).astype(BF16)
    fresh = mm(keys[...], scaled)
    blocks = ROWS // SUB
    entering = [None] * blocks
    state = carry
    for b in range(blocks) if forward else range(blocks - 1, -1, -1):
        half = small[b : b + 1]
        met = half * state
        entering[b] = met.astype(BF16)
        state = half * (met + fresh[b * SUB : (b + 1) * SUB])
    scan = mm(inside[...], scaled) + mm(query[...], jnp.concatenate(entering, axis=0))
    return scan * out + small[8:9] * values


def carry_block(keep, got, core, block, row):
    mine = (core == block // (STEPS // 2)).astype(F32)
    parts = [
        mine * keep[j, row : row + STATE, :].astype(F32)
        + (1.0 - mine) * got[j, row : row + STATE, :].astype(F32)
        for j in range(LANES // TILE)
    ]
    return jnp.concatenate(parts, axis=1)


def grads_kernel(
    cot, other_cot, proj, pack, f_keep, f_got, b_keep, b_got, du_f, du_r, *scratch
):
    step = pl.program_id(0)
    core, _, _, _ = place()
    in_scale, out_scale, rows_scale = scratch[0:3]
    straight, turned = scratch[3:6], scratch[6:9]

    @pl.when(step == 0)
    def _():
        tables = (pack, pack)
        prepare(
            tables, proj, (False, True), (True, True), False, in_scale, out_scale, rows_scale
        )
        prepare_matrices(proj[0], 0, False, *straight)
        prepare_matrices(proj[1], 0, True, *turned)

    back = STEPS - 1 - step
    du_f[...] = scan_block(
        cot[...].astype(F32),
        carry_block(f_keep, f_got, core, step, STATE),
        False,
        spread(2 * TILE, 0, step, False),
        in_scale,
        out_scale,
        rows_scale,
        straight,
    ).astype(BF16)
    mirrored = scan_block(
        other_cot[...].astype(F32),
        carry_block(b_keep, b_got, core, back, 0),
        True,
        spread(2 * TILE, 32, back, True),
        in_scale,
        out_scale,
        rows_scale,
        turned,
    ).astype(BF16)
    du_r[...] = mm(mirrored, exchange_matrix(LANES)).astype(BF16)


def layer_kernel(
    u_f, other_u, proj, pack, other_pack, f_keep, f_got, r_keep, r_got, out, *scratch
):
    step = pl.program_id(0)
    core, _, _, _ = place()
    in_scale, out_scale, rows_scale = scratch[0:3]
    straight, turned = scratch[3:6], scratch[6:9]

    @pl.when(step == 0)
    def _():
        tables = (pack, other_pack)
        prepare(
            tables, proj, (True, False), (False, False), True, in_scale, out_scale, rows_scale
        )
        prepare_matrices(proj[0], STATE, True, *straight)
        prepare_matrices(proj[1], STATE, False, *turned)

    back = STEPS - 1 - step
    y_f = scan_block(
        u_f[...].astype(F32),
        carry_block(f_keep, f_got, core, step, 0),
        True,
        spread(2 * TILE, 0, step, False),
        in_scale,
        out_scale,
        rows_scale,
        straight,
    )
    y_r = scan_block(
        other_u[...].astype(F32),
        carry_block(r_keep, r_got, core, back, 0),
        False,
        spread(2 * TILE, 32, back, False),
        in_scale,
        out_scale,
        rows_scale,
        turned,
    ).astype(BF16)
    out[...] = (y_f + mm(y_r, exchange_matrix(LANES))).astype(BF16)


def scan_scratch():
    square = pltpu.VMEM((ROWS, ROWS), BF16)
    wide = pltpu.VMEM((ROWS, 2 * TILE), BF16)
    return [wide, wide, pltpu.VMEM((16, 2 * TILE), BF16)] + [square] * 6


def carry_specs(rows, mirrored):
    half = STEPS // 2
    if mirrored:
        return [pl.BlockSpec((LANES // TILE, rows, TILE), lambda i: ((STEPS - 1 - i) % half, 0, 0))] * 2
    return [pl.BlockSpec((LANES // TILE, rows, TILE), lambda i: (i % half, 0, 0))] * 2


COLUMNS = pl.BlockSpec((ROWS, LANES), lambda i: (0, i))
MIRRORED = pl.BlockSpec((ROWS, LANES), lambda i: (0, STEPS - 1 - i))
PROJ = pl.BlockSpec((2, ROWS, TILE), lambda i: (0, 0, 0))
PACK = pl.BlockSpec((ROWS + 8, TILE), lambda i: (0, 0))
SCAN_COST = pl.CostEstimate(flops=10 << 30, bytes_accessed=6 << 20, transcendentals=0)


def grads(cot, other_cot, proj, pack, f_carry, b_carry):
    return pl.pallas_call(
        grads_kernel,
        grid=(STEPS,),
        in_specs=[COLUMNS, MIRRORED, PROJ, PACK]
        + carry_specs(2 * STATE, False)
        + carry_specs(STATE, True),
        out_specs=[COLUMNS, COLUMNS],
        out_shape=[shape(ROWS, WIDTH), shape(ROWS, WIDTH)],
        scratch_shapes=scan_scratch(),
        cost_estimate=SCAN_COST,
        name="grads",
    )(cot, other_cot, proj, pack, *f_carry, *b_carry)


def layer(u_f, other_u, proj, pack, other_pack, f_carry, r_carry):
    return pl.pallas_call(
        layer_kernel,
        grid=(STEPS,),
        in_specs=[COLUMNS, MIRRORED, PROJ, PACK, PACK]
        + carry_specs(2 * STATE, False)
        + carry_specs(STATE, True),
        out_specs=COLUMNS,
        out_shape=shape(ROWS, WIDTH),
        scratch_shapes=scan_scratch(),
        cost_estimate=SCAN_COST,
        name="layer",
    )(u_f, other_u, proj, pack, other_pack, *f_carry, *r_carry)


def back_kernel(half, du_f, du_r, direct, mirrored, *rest):
    total = mm_nt(du_f[...], direct[...])
    turn = mm_nt(du_r[...], mirrored[...])
    high = turn.astype(BF16)
    low = (turn - high.astype(F32)).astype(BF16)
    flip = exchange_matrix(LANES)
    total = total + mm(high, flip) + mm(low, flip)
    if len(rest) == 2:
        total = total + rest[0][...].astype(F32)
    rest[-1][...] = total.astype(rest[-1].dtype)


def back(half, du_f, du_r, weight, given=()):
    steps = STEPS // 2
    columns = pl.BlockSpec((ROWS, LANES), lambda i, h: (0, i))
    spec = pltpu.PrefetchScalarGridSpec(
        num_scalar_prefetch=1,
        grid=(steps,),
        in_specs=[
            pl.BlockSpec((ROWS, WIDTH), lambda i, h: (0, 0)),
            pl.BlockSpec((ROWS, WIDTH), lambda i, h: (0, 0)),
            pl.BlockSpec((LANES, WIDTH), lambda i, h: (h[0] * steps + i, 0)),
            pl.BlockSpec((LANES, WIDTH), lambda i, h: (STEPS - 1 - h[0] * steps - i, 0)),
        ]
        + [columns] * len(given),
        out_specs=columns,
    )
    return pl.pallas_call(
        back_kernel,
        grid_spec=spec,
        out_shape=shape(ROWS, WIDTH // 2),
        cost_estimate=pl.CostEstimate(
            flops=2 * ROWS * WIDTH * WIDTH, bytes_accessed=11 << 20, transcendentals=0
        ),
        name="back",
    )(half, du_f, du_r, weight, weight, *given)


def pack_kernel(decay, step, gain, out):
    parts = [decay[0], decay[1], step[0], step[1]]
    out[0:ROWS, :] = jnp.concatenate(parts, axis=0).T
    gains = jnp.concatenate([gain[...]] * 4, axis=1)
    out[ROWS : ROWS + 8, :] = jnp.broadcast_to(gains, (8, TILE))


def pack_table(decay, step, gain):
    return pl.pallas_call(
        pack_kernel,
        out_shape=jax.ShapeDtypeStruct((ROWS + 8, TILE), F32),
        name="pack",
    )(jnp.swapaxes(decay, 1, 2), jnp.swapaxes(step, 1, 2), gain)


def shards(hidden, in_weight, state_proj, log_decay, step_size, skip_gain, cotangent):
    pack = pack_table(log_decay, step_size, skip_gain.reshape(1, 32))
    other_pack = chan_swap(pack)
    other_cot = chan_swap(cotangent)
    u_f, u_r, states = project(hidden, in_weight, state_proj, pack, cotangent)
    keep, send = whole(
        mirror_kernel,
        [shape(SLICES // 2, FULL, TILE)] * 2,
        (cotangent, state_proj, pack, other_pack, states),
        name="mirror",
        flops=8 << 30,
    )
    other_u, f_carry, b_carry, r_carry = carries(keep, send, other_cot, u_r)
    du_f, du_r = grads(cotangent, other_cot, state_proj, pack, f_carry, b_carry)
    here = lax.axis_index("chan").astype(jnp.int32)[None]
    given = chan_swap(back(1 - here, du_f, du_r, in_weight))
    layer_out = layer(u_f, other_u, state_proj, pack, other_pack, f_carry, r_carry)
    input_grad = back(here, du_f, du_r, in_weight, (given,))
    return (layer_out, input_grad)


def solution(mesh):
    in_specs = (
        P("ctx", None),
        P(None, "chan"),
        P(None, "ctx", None),
        P(None, "ctx", "chan"),
        P(None, "ctx", "chan"),
        P("chan"),
        P("ctx", "chan"),
    )
    out_specs = (P("ctx", "chan"), P("ctx", "chan"))
    return jax.shard_map(shards, mesh=mesh, in_specs=in_specs, out_specs=out_specs, check_vma=False)
```

```python
import jax
import jax.numpy as jnp
from jax import lax
from jax.experimental import pallas as pl
from jax.experimental.pallas import tpu as pltpu
from jax.sharding import PartitionSpec as P

F32 = jnp.float32
BF16 = jnp.bfloat16
ROWS = 256
WIDTH = 2048
LANES = 256
STEPS = WIDTH // LANES
HEAD = 64
STATE = 64
SUB = 64
TILE = 128
SLICES = WIDTH // TILE
BODY = 4 * STATE
FULL = BODY + 16
FF, RF, FB, RB = 0, 1, 2, 3
FORWARD = (True, False, False, True)
NT = (((1,), (1,)), ((), ()))


def mm(a, b):
    return jnp.dot(a, b, preferred_element_type=F32)


def mm_nt(a, b):
    return lax.dot_general(a, b, NT, preferred_element_type=F32)


def iota(shape, dim):
    return lax.broadcasted_iota(jnp.int32, shape, dim)


def split3(x):
    high = x.astype(BF16)
    rest = x - high.astype(F32)
    middle = rest.astype(BF16)
    low = (rest - middle.astype(F32)).astype(BF16)
    return high, middle, low


def exact_mm(ones, x):
    high, middle, low = split3(x)
    return mm(ones, high) + mm(ones, middle) + mm(ones, low)


def pair(x):
    high = x.astype(BF16)
    low = (x - high.astype(F32)).astype(BF16)
    return jnp.concatenate([high, low], axis=1)


def exchange_matrix(n):
    return (iota((n, n), 0) + iota((n, n), 1) == n - 1).astype(BF16)


def spread(rows, base, block, mirrored):
    row = iota((rows, LANES), 0) & 127
    head = block * (LANES // HEAD) + iota((rows, LANES), 1) // HEAD
    if mirrored:
        head = WIDTH // HEAD - 1 - head
    return (row == base + head).astype(BF16)


def picks(n, offset):
    row = iota((n, TILE), 0) & (STATE - 1)
    return (iota((n, TILE), 1) == offset + row).astype(BF16)


def place():
    index = lax.axis_index("ctx")
    return index & 1, (index >> 1) & 1, (index >> 2) & 3, index >> 4


def project_kernel(hidden, weight, proj, pack, cot, u_f, u_r, states, both, scale, keys):
    step = pl.program_id(0)

    @pl.when(step == 0)
    def _():
        flip = exchange_matrix(LANES)
        for b in range(STEPS):
            block = hidden[:, b * LANES : (b + 1) * LANES]
            back = STEPS - 1 - b
            both[0:ROWS, b * LANES : (b + 1) * LANES] = block
            both[ROWS : 2 * ROWS, back * LANES : (back + 1) * LANES] = mm(block, flip).astype(BF16)
        table = pack[0:ROWS, :]
        lane = iota((ROWS, TILE), 1)
        decay = jnp.where(lane < 64, table, 0.0)
        lower = (iota((ROWS, ROWS), 0) >= iota((ROWS, ROWS), 1)).astype(BF16)
        total = exact_mm(lower, decay)
        last = total[ROWS - 1 : ROWS, :]
        weight_of = pltpu.roll(table, 64, 1)
        values = jnp.where(
            lane < 32,
            jnp.exp(last - total) * weight_of,
            jnp.where(
                lane < 64, jnp.exp(total - decay) * weight_of, pltpu.roll(jnp.exp(total), 64, 1)
            ),
        )
        scale[...] = pair(values)
        keys[0] = mm_nt(picks(STATE, 0), proj[0]).astype(BF16)
        keys[1] = mm_nt(picks(STATE, 0), proj[1]).astype(BF16)
        keys[2] = mm_nt(picks(STATE, STATE), proj[0]).astype(BF16)

    u = mm(both[...], weight[...]).astype(BF16)
    u_f[...] = u[0:ROWS]
    u_r[...] = u[ROWS : 2 * ROWS]
    values = (u[0:ROWS].astype(F32), u[ROWS : 2 * ROWS].astype(F32), cot[...].astype(F32))
    for scan in range(3):
        wide = mm(scale[...], spread(2 * TILE, 32 * scan, step, False))
        state = mm(keys[scan], (values[scan] * wide).astype(BF16)).astype(BF16)
        for j in range(LANES // TILE):
            states[j, scan * STATE : (scan + 1) * STATE, :] = state[:, j * TILE : (j + 1) * TILE]


def project(hidden, weight, proj, pack, cot):
    columns = pl.BlockSpec((ROWS, LANES), lambda i: (0, i))
    return pl.pallas_call(
        project_kernel,
        grid=(STEPS,),
        in_specs=[
            pl.BlockSpec((ROWS, WIDTH), lambda i: (0, 0)),
            pl.BlockSpec((WIDTH, LANES), lambda i: (0, i)),
            pl.BlockSpec((2, ROWS, TILE), lambda i: (0, 0, 0)),
            pl.BlockSpec((ROWS + 8, TILE), lambda i: (0, 0)),
            columns,
        ],
        out_specs=[
            columns,
            columns,
            pl.BlockSpec((LANES // TILE, 3 * STATE, TILE), lambda i: (i, 0, 0)),
        ],
        out_shape=[
            jax.ShapeDtypeStruct((ROWS, WIDTH), BF16),
            jax.ShapeDtypeStruct((ROWS, WIDTH), BF16),
            jax.ShapeDtypeStruct((SLICES, 3 * STATE, TILE), BF16),
        ],
        scratch_shapes=[
            pltpu.VMEM((2 * ROWS, WIDTH), BF16),
            pltpu.VMEM((ROWS, 2 * TILE), BF16),
            pltpu.VMEM((3, STATE, ROWS), BF16),
        ],
        cost_estimate=pl.CostEstimate(
            flops=4 * ROWS * WIDTH * WIDTH, bytes_accessed=14 << 20, transcendentals=0
        ),
        name="project",
    )(hidden, weight, proj, pack, cot)


def mirror_kernel(cot, proj, pack, other_pack, states, keep, send):
    core, _, _, _ = place()
    decay = jnp.where(iota((ROWS, TILE), 1) < 64, other_pack[0:ROWS, :], 0.0)
    own = jnp.where(iota((ROWS, TILE), 1) < 64, pack[0:ROWS, :], 0.0)
    lower = (iota((ROWS, ROWS), 0) >= iota((ROWS, ROWS), 1)).astype(BF16)
    total = exact_mm(lower, decay)
    last = total[ROWS - 1 : ROWS, :]
    scale = pair(jnp.exp(last - total + decay))
    keys = mm_nt(picks(STATE, STATE), proj[1]).astype(BF16)
    own_last = exact_mm(jnp.ones((16, ROWS), BF16), own)
    other_last = jnp.broadcast_to(last, (16, TILE))
    row, lane = iota((16, TILE), 0), iota((16, TILE), 1)
    scan, part = row // 3, row % 3

    def parts(x, wanted):
        high, middle, low = split3(jnp.exp(x))
        chosen = jnp.where(
            part == 0, high.astype(F32), jnp.where(part == 1, middle.astype(F32), low.astype(F32))
        )
        return jnp.where(wanted, chosen, 0.0).astype(BF16)

    direction = lane // 32
    own_rows = parts(own_last, (scan < 3) & (direction == (scan == RF).astype(jnp.int32)))
    other_rows = parts(other_last, (scan == RB) & (direction == 1))
    head_row = iota((TILE, LANES), 0) & 31
    for b in range(STEPS):
        head = b * (LANES // HEAD) + iota((TILE, LANES), 1) // HEAD
        straight = (head_row == head).astype(BF16)
        turned = (head_row == WIDTH // HEAD - 1 - head).astype(BF16)
        decays = (mm(own_rows, straight) + mm(other_rows, turned)).astype(BF16)
        wide = mm(scale, spread(2 * TILE, 32, b, True))
        block = cot[:, b * LANES : (b + 1) * LANES].astype(F32)
        state = mm(keys, (block * wide).astype(BF16)).astype(BF16)
        for j in range(LANES // TILE):
            s = b * (LANES // TILE) + j
            half, at = s // (SLICES // 2), s % (SLICES // 2)
            columns = slice(j * TILE, (j + 1) * TILE)

            def write(out):
                out[at, 0 : 3 * STATE, :] = states[s]
                out[at, 3 * STATE : BODY, :] = state[:, columns]
                out[at, BODY:FULL, :] = decays[:, columns]

            @pl.when(core == half)
            def _():
                write(keep)

            @pl.when(core != half)
            def _():
                write(send)


def whole(kernel, outs, args, scratch=(), name=None, flops=0, after=(), through=()):
    bytes_accessed = sum(a.size * a.dtype.itemsize for a in args)
    bytes_accessed += sum(2 * o.size for o in outs)
    first = len(args)
    start = first + len(after) + len(through)
    end = start + len(outs)

    def body(*refs):
        kernel(*refs[:first], *refs[start:end], *refs[end + len(through) :])

    there = [pl.BlockSpec(memory_space=pl.ANY)]
    return pl.pallas_call(
        body,
        out_shape=list(outs) + [jax.ShapeDtypeStruct(t.shape, t.dtype) for t in through],
        in_specs=[pl.BlockSpec(memory_space=pltpu.VMEM)] * len(args)
        + there * (len(after) + len(through)),
        out_specs=[pl.BlockSpec(memory_space=pltpu.VMEM)] * len(outs) + there * len(through),
        input_output_aliases={first + len(after) + i: len(outs) + i for i in range(len(through))},
        scratch_shapes=list(scratch),
        cost_estimate=pl.CostEstimate(
            flops=flops, bytes_accessed=bytes_accessed, transcendentals=0
        ),
        name=name,
    )(*args, *after, *through)


def shape(*dims):
    return jax.ShapeDtypeStruct(dims, BF16)


def read_decays(tile):
    tile = tile.astype(F32)
    return [
        tile[3 * i : 3 * i + 1] + tile[3 * i + 1 : 3 * i + 2] + tile[3 * i + 2 : 3 * i + 3]
        for i in range(tile.shape[0] // 4)
    ]


def decay_rows(decays):
    row = iota((16, TILE), 0)
    out = jnp.zeros((16, TILE), F32)
    for i, d in enumerate(decays):
        for j, p in enumerate(split3(d)):
            out = jnp.where(row == 3 * i + j, p.astype(F32), out)
    return out.astype(BF16)


def rows_of(scan):
    return slice(scan * STATE, (scan + 1) * STATE)


def pair_total(own, got, at, first, out, to):
    mine, theirs = read_decays(own[at, BODY:FULL, :]), read_decays(got[at, BODY:FULL, :])
    for scan in range(4):
        early = first if FORWARD[scan] else 1.0 - first
        alpha = early * theirs[scan] + (1.0 - early)
        beta = early + (1.0 - early) * mine[scan]
        out[to, rows_of(scan), :] = (
            alpha * own[at, rows_of(scan), :].astype(F32)
            + beta * got[at, rows_of(scan), :].astype(F32)
        ).astype(BF16)
    out[to, BODY:FULL, :] = decay_rows([a * b for a, b in zip(mine, theirs)])


def pair_carry(own, got, at, first, carry, mine, theirs, scan):
    early = first if FORWARD[scan] else 1.0 - first
    here = (1.0 - early) * (theirs[scan] * carry + got[at, rows_of(scan), :].astype(F32))
    here = here + early * carry
    there = early * (mine[scan] * carry + own[at, rows_of(scan), :].astype(F32))
    there = there + (1.0 - early) * carry
    return here.astype(BF16), there.astype(BF16)


def core_up_kernel(own, got, keep, send):
    core, x, _, _ = place()
    first = 1.0 - core.astype(F32)

    @pl.loop(0, 4)
    def _(j):
        pair_total(own, got, x * 4 + j, first, keep, j)
        pair_total(own, got, (1 - x) * 4 + j, first, send, j)


def x_up_kernel(own, got, *outs):
    _, x, y, _ = place()
    first = 1.0 - x.astype(F32)
    for k in range(4):
        pair_total(own, got, (y + k) & 3, first, outs[k], 0)


def y_total_kernel(a0, a1, a2, a3, z1, z2, z3, stack, total):
    _, _, y, z = place()
    for k, a in enumerate((a0, a1, a2, a3)):
        stack[(y - k) & 3] = a[0]
    decays = [read_decays(stack[p, BODY:FULL, :]) for p in range(4)]
    for scan in range(4):
        order = (0, 1, 2, 3) if FORWARD[scan] else (3, 2, 1, 0)
        t = stack[order[0], rows_of(scan), :].astype(F32)
        for p in order[1:]:
            t = decays[p][scan] * t + stack[p, rows_of(scan), :].astype(F32)
        total[rows_of(scan), :] = t.astype(BF16)
    product = [decays[0][s] * decays[1][s] * decays[2][s] * decays[3][s] for s in range(4)]
    later = decay_rows([product[FF], product[RB]])
    earlier = decay_rows([product[RF], product[FB]])
    for k, out in enumerate((z1, z2, z3)):

        @pl.when(z + k + 1 < 4)
        def _():
            out[0:STATE, :] = total[rows_of(FF), :]
            out[STATE : 2 * STATE, :] = total[rows_of(RB), :]
            out[2 * STATE :, :] = later

        @pl.when(z + k + 1 >= 4)
        def _():
            out[0:STATE, :] = total[rows_of(RF), :]
            out[STATE : 2 * STATE, :] = total[rows_of(FB), :]
            out[2 * STATE :, :] = earlier


def z_carry_kernel(a0, a1, a2, a3, q1, q2, q3, d0, d1, d2, d3, stack, out):
    _, _, y, z = place()
    for k, a in enumerate((a0, a1, a2, a3)):
        stack[(y - k) & 3] = a[0]
    decays = [read_decays(stack[p, BODY:FULL, :]) for p in range(4)]
    got = (q1, q2, q3)
    plane = [read_decays(q[2 * STATE :, :]) for q in got]
    before = [(z >= k).astype(F32) for k in (1, 2, 3)]
    for scan in range(4):
        half = 0 if scan in (FF, RF) else 1
        part = [q[half * STATE : (half + 1) * STATE, :].astype(F32) for q in got]
        d = [p[half] for p in plane]
        if FORWARD[scan]:
            m = before
            order, positions = (0, 1, 2), (0, 1, 2, 3)
        else:
            m = [1.0 - b for b in before]
            order, positions = (2, 1, 0), (3, 2, 1, 0)
        i, j, k = order
        c = m[i] * (part[i] + d[i] * (m[j] * (part[j] + d[j] * (m[k] * part[k]))))
        for p in positions:
            out[p, rows_of(scan), :] = c.astype(BF16)
            if p != positions[-1]:
                c = decays[p][scan] * c + stack[p, rows_of(scan), :].astype(F32)
    for k, d in enumerate((d0, d1, d2, d3)):
        d[...] = out[(y - k) & 3]


def x_down_kernel(c0, c1, c2, c3, own, got, keep, send):
    _, x, y, _ = place()
    first = 1.0 - x.astype(F32)
    for k, c in enumerate((c0, c1, c2, c3)):
        at = (y + k) & 3
        mine, theirs = read_decays(own[at, BODY:FULL, :]), read_decays(got[at, BODY:FULL, :])
        for scan in range(4):
            here, there = pair_carry(
                own, got, at, first, c[rows_of(scan), :].astype(F32), mine, theirs, scan
            )
            keep[at, rows_of(scan), :] = here
            send[at, rows_of(scan), :] = there


def core_down_kernel(c_own, c_got, own, got, f_keep, f_send, b_same, b_cross, r_same, r_cross):
    core, x, _, _ = place()
    first = 1.0 - core.astype(F32)

    @pl.loop(0, 4)
    def _(j):
        for carry, side in ((c_own, x), (c_got, 1 - x)):
            at = side * 4 + j
            mine, theirs = read_decays(own[at, BODY:FULL, :]), read_decays(got[at, BODY:FULL, :])
            for scan, here_out, there_out, row in (
                (FF, f_keep, f_send, 0),
                (FB, f_keep, f_send, STATE),
                (RB, b_same, b_cross, 0),
                (RF, r_same, r_cross, 0),
            ):
                here, there = pair_carry(
                    own,
                    got,
                    at,
                    first,
                    carry[j, rows_of(scan), :].astype(F32),
                    mine,
                    theirs,
                    scan,
                )
                here_out[at, row : row + STATE, :] = here
                there_out[at, row : row + STATE, :] = there


def ctx_permute(x, target):
    return lax.ppermute(x, "ctx", [(i, target(i)) for i in range(64)])


def core_swap(x):
    return ctx_permute(x, lambda i: i ^ 1)


def x_swap(x):
    return ctx_permute(x, lambda i: i ^ 2)


def y_shift(x, k):
    return ctx_permute(x, lambda i: (i & ~12) | ((i + 4 * k) & 12))


def z_shift(x, k):
    return ctx_permute(x, lambda i: (i + 16 * k) & 63)


def chan_swap(x):
    return lax.ppermute(x, "chan", [(0, 1), (1, 0)])


def cross_swap(x):
    return lax.ppermute(x, ("ctx", "chan"), [(i, i ^ 3) for i in range(128)])


def carries(keep1, send1, other_cot, u_r, grads_tables, layer_tables):
    slices = SLICES // 2
    got1 = core_swap(send1)
    keep2, send2 = whole(
        core_up_kernel,
        [shape(4, FULL, TILE)] * 2,
        (keep1, got1),
        name="core_up",
        after=(other_cot,),
    )
    got2 = x_swap(send2)
    *tops, u_r = whole(
        x_up_kernel,
        [shape(1, FULL, TILE)] * 4,
        (keep2, got2),
        name="x_up",
        after=(grads_tables[2],),
        through=(u_r,),
    )
    other_u = chan_swap(u_r)
    row = [tops[0]] + [y_shift(tops[k], k) for k in (1, 2, 3)]
    stack = pltpu.VMEM((4, FULL, TILE), BF16)
    planes = whole(
        y_total_kernel,
        [shape(2 * STATE + 16, TILE)] * 3,
        row,
        [stack, pltpu.VMEM((BODY, TILE), BF16)],
        name="y_total",
    )
    other = [z_shift(planes[k - 1], k) for k in (1, 2, 3)]
    down = whole(
        z_carry_kernel,
        [shape(BODY, TILE)] * 4,
        row + other,
        [stack, pltpu.VMEM((4, BODY, TILE), BF16)],
        name="z_carry",
    )
    down = [down[0]] + [y_shift(down[k], -k) for k in (1, 2, 3)]
    keep3, send3 = whole(
        x_down_kernel,
        [shape(4, BODY, TILE)] * 2,
        [*down, keep2, got2],
        name="x_down",
        after=(other_u,),
    )
    got3 = x_swap(send3)
    f_keep, f_send, b_same, b_cross, r_same, r_cross = whole(
        core_down_kernel,
        [shape(slices, 2 * STATE, TILE)] * 2 + [shape(slices, STATE, TILE)] * 4,
        (keep3, got3, keep1, got1),
        name="core_down",
        after=(layer_tables[2],),
    )
    return (
        other_u,
        (f_keep, core_swap(f_send)),
        (chan_swap(b_same), cross_swap(b_cross)),
        (chan_swap(r_same), cross_swap(r_cross)),
    )


def prepare(tables, proj_of, forward, exclusive, with_weight, in_scale, out_scale, rows_scale):
    lane = iota((ROWS, TILE), 1)
    first, second = tables
    table = jnp.where(lane & 32 == 0, first[0:ROWS, :], second[0:ROWS, :])
    decay = jnp.where(lane < 64, table, 0.0)
    weight = pltpu.roll(table, 64, 1)
    row, column = iota((ROWS, ROWS), 0), iota((ROWS, ROWS), 1)
    same = row // SUB == column // SUB
    total = exact_mm((same & (row >= column)).astype(BF16), decay)
    full = exact_mm(same.astype(BF16), decay)

    def level(i):
        c = total if forward[i] else full - total + decay
        return c - decay if exclusive[i] else c

    rise = jnp.where(lane < 32, level(0), level(1)) - 0.5 * full
    in_scale[...] = pair(jnp.exp(-rise) * weight if with_weight else jnp.exp(-rise))
    out_scale[...] = pair(jnp.exp(rise) if with_weight else jnp.exp(rise) * weight)
    small = iota((16, TILE), 0)
    tail = jnp.where(
        iota((8, TILE), 1) & 32 == 0, first[ROWS : ROWS + 8, :], second[ROWS : ROWS + 8, :]
    )
    half = jnp.exp(0.5 * full)
    values = jnp.broadcast_to(tail[0:1], (16, TILE))
    for b in range(ROWS // SUB):
        values = jnp.where(small == b, half[b * SUB : b * SUB + 1], values)
    rows_scale[...] = pair(values)


def prepare_matrices(proj, query_at, forward, inside, query, keys):
    key_at = STATE - query_at
    row, column = iota((ROWS, ROWS), 0), iota((ROWS, ROWS), 1)
    same = row // SUB == column // SUB
    order = (row >= column) if forward else (row <= column)
    tiled_query = mm_nt(proj, picks(ROWS, query_at))
    tiled_keys = mm_nt(picks(ROWS, key_at), proj)
    q = jnp.where(iota((ROWS, TILE), 1) // STATE == query_at // STATE, proj.astype(F32), 0.0)
    swapped = pltpu.roll(proj.astype(F32), STATE, 1).astype(BF16)
    affinity = mm_nt(q.astype(BF16), swapped)
    inside[...] = jnp.where(same & order, affinity, 0.0).astype(BF16)
    query[...] = jnp.where(same, tiled_query, 0.0).astype(BF16)
    keys[...] = jnp.where(same, tiled_keys, 0.0).astype(BF16)


def scan_block(values, carry, forward, lanes, in_scale, out_scale, rows_scale, mats):
    inside, query, keys = mats
    wide = mm(in_scale[...], lanes)
    small = mm(rows_scale[...], lanes)
    out = mm(out_scale[...], lanes)
    scaled = (values * wide).astype(BF16)
    fresh = mm(keys[...], scaled)
    blocks = ROWS // SUB
    entering = [None] * blocks
    state = carry
    for b in range(blocks) if forward else range(blocks - 1, -1, -1):
        half = small[b : b + 1]
        met = half * state
        entering[b] = met.astype(BF16)
        state = half * (met + fresh[b * SUB : (b + 1) * SUB])
    scan = mm(inside[...], scaled) + mm(query[...], jnp.concatenate(entering, axis=0))
    return scan * out + small[8:9] * values


def carry_block(keep, got, core, block, row):
    mine = (core == block // (STEPS // 2)).astype(F32)
    parts = [
        mine * keep[j, row : row + STATE, :].astype(F32)
        + (1.0 - mine) * got[j, row : row + STATE, :].astype(F32)
        for j in range(LANES // TILE)
    ]
    return jnp.concatenate(parts, axis=1)


def grads_tables_kernel(proj, pack, *out):
    prepare((pack, pack), proj, (False, True), (True, True), False, *out[0:3])
    prepare_matrices(proj[0], 0, False, *out[3:6])
    prepare_matrices(proj[1], 0, True, *out[6:9])


def layer_tables_kernel(proj, pack, other_pack, *out):
    prepare((pack, other_pack), proj, (True, False), (False, False), True, *out[0:3])
    prepare_matrices(proj[0], STATE, True, *out[3:6])
    prepare_matrices(proj[1], STATE, False, *out[6:9])


def grads_kernel(
    cot, other_cot, f_keep, f_got, b_keep, b_got, *refs
):
    step = pl.program_id(0)
    core, _, _, _ = place()
    in_scale, out_scale, rows_scale = refs[0:3]
    straight, turned = refs[3:6], refs[6:9]
    du_f, du_r = refs[9:]
    back = STEPS - 1 - step
    du_f[...] = scan_block(
        cot[...].astype(F32),
        carry_block(f_keep, f_got, core, step, STATE),
        False,
        spread(2 * TILE, 0, step, False),
        in_scale,
        out_scale,
        rows_scale,
        straight,
    ).astype(BF16)
    mirrored = scan_block(
        other_cot[...].astype(F32),
        carry_block(b_keep, b_got, core, back, 0),
        True,
        spread(2 * TILE, 32, back, True),
        in_scale,
        out_scale,
        rows_scale,
        turned,
    ).astype(BF16)
    du_r[...] = mm(mirrored, exchange_matrix(LANES)).astype(BF16)


def layer_kernel(
    u_f, other_u, f_keep, f_got, r_keep, r_got, *refs
):
    step = pl.program_id(0)
    core, _, _, _ = place()
    in_scale, out_scale, rows_scale = refs[0:3]
    straight, turned = refs[3:6], refs[6:9]
    out = refs[9]
    back = STEPS - 1 - step
    y_f = scan_block(
        u_f[...].astype(F32),
        carry_block(f_keep, f_got, core, step, 0),
        True,
        spread(2 * TILE, 0, step, False),
        in_scale,
        out_scale,
        rows_scale,
        straight,
    )
    y_r = scan_block(
        other_u[...].astype(F32),
        carry_block(r_keep, r_got, core, back, 0),
        False,
        spread(2 * TILE, 32, back, False),
        in_scale,
        out_scale,
        rows_scale,
        turned,
    ).astype(BF16)
    out[...] = (y_f + mm(y_r, exchange_matrix(LANES))).astype(BF16)


TABLES = [shape(ROWS, 2 * TILE)] * 2 + [shape(16, 2 * TILE)] + [shape(ROWS, ROWS)] * 6
TABLE_SPECS = [pl.BlockSpec(t.shape, lambda i: (0, 0)) for t in TABLES]


def carry_specs(rows, mirrored):
    half = STEPS // 2
    if mirrored:
        return [pl.BlockSpec((LANES // TILE, rows, TILE), lambda i: ((STEPS - 1 - i) % half, 0, 0))] * 2
    return [pl.BlockSpec((LANES // TILE, rows, TILE), lambda i: (i % half, 0, 0))] * 2


COLUMNS = pl.BlockSpec((ROWS, LANES), lambda i: (0, i))
MIRRORED = pl.BlockSpec((ROWS, LANES), lambda i: (0, STEPS - 1 - i))
SCAN_COST = pl.CostEstimate(flops=10 << 30, bytes_accessed=6 << 20, transcendentals=0)


def grads(cot, other_cot, tables, f_carry, b_carry):
    return pl.pallas_call(
        grads_kernel,
        grid=(STEPS,),
        in_specs=[COLUMNS, MIRRORED]
        + carry_specs(2 * STATE, False)
        + carry_specs(STATE, True)
        + TABLE_SPECS,
        out_specs=[COLUMNS, COLUMNS],
        out_shape=[shape(ROWS, WIDTH), shape(ROWS, WIDTH)],
        cost_estimate=SCAN_COST,
        name="grads",
    )(cot, other_cot, *f_carry, *b_carry, *tables)


def layer(u_f, other_u, tables, f_carry, r_carry):
    return pl.pallas_call(
        layer_kernel,
        grid=(STEPS,),
        in_specs=[COLUMNS, MIRRORED]
        + carry_specs(2 * STATE, False)
        + carry_specs(STATE, True)
        + TABLE_SPECS,
        out_specs=COLUMNS,
        out_shape=shape(ROWS, WIDTH),
        cost_estimate=SCAN_COST,
        name="layer",
    )(u_f, other_u, *f_carry, *r_carry, *tables)


def back_kernel(half, du_f, du_r, direct, mirrored, *rest):
    total = mm_nt(du_f[...], direct[...])
    turn = mm_nt(du_r[...], mirrored[...])
    high = turn.astype(BF16)
    low = (turn - high.astype(F32)).astype(BF16)
    flip = exchange_matrix(LANES)
    total = total + mm(high, flip) + mm(low, flip)
    if len(rest) == 2:
        total = total + rest[0][...].astype(F32)
    rest[-1][...] = total.astype(rest[-1].dtype)


def back(half, du_f, du_r, weight, given=()):
    steps = STEPS // 2
    columns = pl.BlockSpec((ROWS, LANES), lambda i, h: (0, i))
    spec = pltpu.PrefetchScalarGridSpec(
        num_scalar_prefetch=1,
        grid=(steps,),
        in_specs=[
            pl.BlockSpec((ROWS, WIDTH), lambda i, h: (0, 0)),
            pl.BlockSpec((ROWS, WIDTH), lambda i, h: (0, 0)),
            pl.BlockSpec((LANES, WIDTH), lambda i, h: (h[0] * steps + i, 0)),
            pl.BlockSpec((LANES, WIDTH), lambda i, h: (STEPS - 1 - h[0] * steps - i, 0)),
        ]
        + [columns] * len(given),
        out_specs=columns,
    )
    return pl.pallas_call(
        back_kernel,
        grid_spec=spec,
        out_shape=shape(ROWS, WIDTH // 2),
        cost_estimate=pl.CostEstimate(
            flops=2 * ROWS * WIDTH * WIDTH, bytes_accessed=11 << 20, transcendentals=0
        ),
        name="back",
    )(half, du_f, du_r, weight, weight, *given)


def pack_kernel(decay, step, gain, out):
    parts = [decay[0], decay[1], step[0], step[1]]
    out[0:ROWS, :] = jnp.concatenate(parts, axis=0).T
    gains = jnp.concatenate([gain[...]] * 4, axis=1)
    out[ROWS : ROWS + 8, :] = jnp.broadcast_to(gains, (8, TILE))


def pack_table(decay, step, gain):
    return pl.pallas_call(
        pack_kernel,
        out_shape=jax.ShapeDtypeStruct((ROWS + 8, TILE), F32),
        name="pack",
    )(jnp.swapaxes(decay, 1, 2), jnp.swapaxes(step, 1, 2), gain)


def shards(hidden, in_weight, state_proj, log_decay, step_size, skip_gain, cotangent):
    pack = pack_table(log_decay, step_size, skip_gain.reshape(1, 32))
    other_pack = chan_swap(pack)
    other_cot = chan_swap(cotangent)
    u_f, u_r, states = project(hidden, in_weight, state_proj, pack, cotangent)
    keep, send = whole(
        mirror_kernel,
        [shape(SLICES // 2, FULL, TILE)] * 2,
        (cotangent, state_proj, pack, other_pack, states),
        name="mirror",
        flops=8 << 30,
    )
    grads_tables = whole(
        grads_tables_kernel, TABLES, (state_proj, pack), name="grads_tables", flops=1 << 30
    )
    layer_tables = whole(
        layer_tables_kernel,
        TABLES,
        (state_proj, pack, other_pack),
        name="layer_tables",
        flops=1 << 30,
    )
    other_u, f_carry, b_carry, r_carry = carries(
        keep, send, other_cot, u_r, grads_tables, layer_tables
    )
    du_f, du_r = grads(cotangent, other_cot, grads_tables, f_carry, b_carry)
    here = lax.axis_index("chan").astype(jnp.int32)[None]
    given = chan_swap(back(1 - here, du_f, du_r, in_weight))
    layer_out = layer(u_f, other_u, layer_tables, f_carry, r_carry)
    input_grad = back(here, du_f, du_r, in_weight, (given,))
    return (layer_out, input_grad)


def solution(mesh):
    in_specs = (
        P("ctx", None),
        P(None, "chan"),
        P(None, "ctx", None),
        P(None, "ctx", "chan"),
        P(None, "ctx", "chan"),
        P("chan"),
        P("ctx", "chan"),
    )
    out_specs = (P("ctx", "chan"), P("ctx", "chan"))
    return jax.shard_map(shards, mesh=mesh, in_specs=in_specs, out_specs=out_specs, check_vma=False)
```
